256 devices in a mesh: dp: 32 (over y, z_lo, core), cent: 8 (over x, z_hi).
Axes of the slice: x: 4, y: 4, z: 8 (z_hi: 2, z_lo: 4; z = z_hi * 4 + z_lo), core: 2. Of those that a mesh axis runs over, the one named last changes fastest.
Arguments:
- hidden: bfloat16 [5632, 11008], P('dp', 'cent'), may hold values from -6 to 6
- residual: bfloat16 [5632, 4096], P('dp', 'cent'), may hold values from -6 to 6
- down_weight: bfloat16 [11008, 4096], P('cent', 'dp'), may hold values from -0.0546875 to 0.0546875
- gain: float32 [4096], P('cent'), may hold values from 0.1 to 1.9
- proj_weight: bfloat16 [4096, 1024], P('cent'), may hold values from -0.09375 to 0.09375
- centroids: bfloat16 [131072, 1024], P(('dp', 'cent')), may hold values from -24 to 24
Outputs:
- weighted: float32 [131072, 1024], P(('dp', 'cent'))
- counts: float32 [131072], P(('dp', 'cent'))
The draws below stay inside these ranges and needn't reach their ends.
All inputs are finite; a program needn't handle non-finite values.
Results may differ from the reference program's by a relative error of at most 0.011.
Values may be sent and summed in bfloat16 or wider, within the bound.
A program may use at most 128 MiB of HBM per device.

```python
import math
import jax
import jax.numpy as jnp
from jax import lax

D = 4096
FF = 11008
E = 1024
CENT_DEV = 512
PASSAGES = 5632
CENTROIDS = 131072


def draw_centroids(key, part):
    key_base = jax.random.fold_in(key, 0)
    normal_base = jax.random.normal(key_base, (CENTROIDS, E), jnp.float32)
    row_scale = jnp.full((CENTROIDS, 1), 0.15, jnp.float32)
    return jnp.clip(normal_base * row_scale, -24.0, 24.0).astype(jnp.bfloat16)


def block_scale(rng, dims, cuts, least, high):
    factor_of = 1.0
    for dim, blocks in cuts:
        steps = jax.random.uniform(jax.random.fold_in(jax.random.fold_in(rng, 6), dim), (blocks,), jnp.float32, least / len(cuts), high / len(cuts))
        factor_of = factor_of * jnp.repeat(jnp.exp(steps), dims[dim] // blocks).reshape((-1,) + (1,) * (len(dims) - 1 - dim))
    return factor_of


def scatter_about(key, shape, spread, bound, cuts=(), kind=jnp.bfloat16):
    factor_of = block_scale(key, shape, cuts, -0.22, 0.18) if cuts else 1.0
    values = jax.random.normal(key, shape, jnp.float32) * spread * factor_of
    return jnp.minimum(jnp.maximum(values, -bound), bound).astype(kind)


def setup_inputs(seed: int = 0) -> dict:
    seeds = jax.random.split(jax.random.key(seed), 7)
    return {
        "hidden": scatter_about(seeds[0], (PASSAGES, FF), 1.0, 6.0, ((0, 32), (1, 8))),
        "residual": scatter_about(seeds[1], (PASSAGES, D), 1.0, 6.0, ((0, 32), (1, 8))),
        "down_weight": scatter_about(seeds[2], (FF, D), FF ** -0.5, 0.0546875, ((0, 8), (1, 32))),
        "gain": jnp.clip(1.0 + 0.18 * jax.random.normal(seeds[3], (D,), jnp.float32), 0.1, 1.9),
        "proj_weight": scatter_about(seeds[4], (D, E), D ** -0.5, 0.09375, ((0, 8),)),
        "centroids": draw_centroids(jax.random.fold_in(seeds[6], 71), 0),
    }


def reference(hidden, residual, down_weight, gain, proj_weight, centroids):
    layer_out = jnp.dot(hidden, down_weight, preferred_element_type=jnp.float32) + residual.astype(jnp.float32)
    normed = (layer_out * gain).astype(jnp.bfloat16)
    raw_embed = jnp.dot(normed, proj_weight, preferred_element_type=jnp.float32)
    embed = (raw_embed * lax.rsqrt(lax.optimization_barrier(jnp.mean(raw_embed * raw_embed, axis=1, keepdims=True)) + 1e-06)).astype(jnp.bfloat16)
    inverse = 1.0 / (math.sqrt(E) * 0.05)
    blocks = centroids.reshape(CENTROIDS // CENT_DEV, CENT_DEV, E)

    def max_pass(carry, block_rows):
        run_max, run_total = carry
        scores = jnp.dot(embed, block_rows.T, preferred_element_type=jnp.float32) * inverse
        new_max = jnp.maximum(run_max, lax.optimization_barrier(jnp.max(scores, axis=1)))
        new_total = run_total * jnp.exp(run_max - new_max) + lax.optimization_barrier(jnp.sum(jnp.exp(scores - new_max[:, None]), axis=1))
        return ((new_max, new_total), None)
    start = (jnp.full((PASSAGES,), -jnp.inf, jnp.float32), jnp.zeros((PASSAGES,), jnp.float32))
    (row_max, row_total), _ = lax.scan(max_pass, start, blocks)
    log_total = row_max + jnp.log(row_total)
    scale_up = CENTROIDS / PASSAGES

    def sum_pass(block_rows):
        scores = jnp.dot(embed, block_rows.T, preferred_element_type=jnp.float32) * inverse
        probability = jnp.exp(scores - log_total[:, None])
        block_counts = scale_up * lax.optimization_barrier(jnp.sum(probability, axis=0))
        prob_low = probability.astype(jnp.bfloat16)
        block_sums = scale_up * jnp.dot(prob_low.T, embed, preferred_element_type=jnp.float32)
        return (block_sums, block_counts)
    weighted, counts = lax.map(sum_pass, blocks)
    return (weighted.reshape(CENTROIDS, E), counts.reshape(CENTROIDS))
```

```python
import functools
import math

import jax
import jax.numpy as jnp
from jax import lax
from jax.experimental import pallas as pl
from jax.experimental.pallas import tpu as pltpu
from jax.sharding import PartitionSpec as P

MESH = pl.DeviceIdType.MESH
NX, NY, NZ = 4, 4, 8
NL = 4
LANES = 128


def coordinates():
    dp, cent = lax.axis_index("dp"), lax.axis_index("cent")
    y, low, core = dp // (2 * NL), (dp // 2) % NL, dp % 2
    return cent // 2, y, (cent % 2) * NL + low, core


def device(x, y, z, core):
    return (y * (2 * NL) + (z % NL) * 2 + core, x * 2 + z // NL)


def aligned(value, multiple):
    return pl.multiple_of(value, multiple)


def greet(peers):
    barrier = pltpu.get_barrier_semaphore()
    for peer in peers:
        pl.semaphore_signal(barrier, inc=1, device_id=peer, device_id_type=MESH)
    pl.semaphore_wait(barrier, len(peers))


def gather_plan(rows, x, y, z):
    low, high = z % NL, z // NL
    r0, r1, r2 = rows
    b0, b1, b2 = 0, 16 * r0, 16 * (r0 + r1)

    def box(row, count, col, width):
        return (aligned(row, 16), count, aligned(col, LANES), width)

    def column(zc, xc):
        return ((zc // NL) * NX + xc) * LANES

    first = (
        ("x", lambda i: [box(b0 + (low * NY + y) * r0, r0, (high * NX + i) * LANES, LANES)]),
        ("y", lambda i: [box(b0 + (low * NY + i) * r0, r0, high * NX * LANES, NX * LANES)]),
        ("z", lambda i: [box(b0 + (i % NL) * NY * r0, NY * r0, (i // NL) * NX * LANES, NX * LANES)]),
    )
    second = (
        ("y", lambda i: [box(b1 + (low * NY + i) * r1, r1, column(z, x), LANES)]),
        ("z", lambda i: [box(b1 + (i % NL) * NY * r1, NY * r1, column(i, x), LANES)]),
        ("x", lambda i: [box(b1, 16 * r1, (h * NX + i) * LANES, LANES) for h in range(2)]),
    )
    third = (
        ("z", lambda i: [box(b2 + (y * NL + i % NL) * r2, r2, column(i, x), LANES)]),
        ("x", lambda i: [box(b2 + y * NL * r2, NL * r2, (h * NX + i) * LANES, LANES) for h in range(2)]),
        ("y", lambda i: [box(b2 + i * NL * r2, NL * r2, 0, 2 * NX * LANES)]),
    )
    own = (
        (0, r0, aligned(b0 + (low * NY + y) * r0, 16)),
        (r0, r1, aligned(b1 + (low * NY + y) * r1, 16)),
        (r0 + r1, r2, aligned(b2 + (y * NL + low) * r2, 16)),
    )
    return (first, second, third), own, aligned(column(z, x), LANES)


def half(box, which):
    row, count, col, width = box
    upper = (count // 2 + 15) // 16 * 16
    return (row, upper, col, width) if which == 0 else (aligned(row + upper, 16), count - upper, col, width)


def ring_steps(stages, position, size):
    steps = []
    for axis, boxes in stages:
        n, me = size[axis], position[axis]
        for s in range(1, n // 2 + 1):
            sends = []
            for which, way in ((0, 1), (1, -1)):
                sent = boxes((me - way * (s - 1) + n) % n)
                got = boxes((me - way * s + n) % n)
                if s == n // 2:
                    sent, got = [half(b, which) for b in sent], [half(b, which) for b in got]
                sends.append((way, axis, sent, got))
            steps.append(sends)
    return steps


def main_kernel(
    rows, chunk, inverse, scale_up,
    block_ref, cent_ref, weighted_ref, counts_ref,
    embed, cents, expo, prob, maxima, logs, total, heard, other_sum, own_sum, other_count, sent_count,
    send_sem, recv_sem, local_sem, cent_sem, lse_send, lse_recv, out_sem,
):
    x, y, z, core = coordinates()
    here = {"x": x, "y": y, "z": z}
    size = {"x": NX, "y": NY, "z": NZ}

    def at(axis, value):
        place = dict(here)
        place[axis] = value
        return device(place["x"], place["y"], place["z"], core)

    mate = device(x, y, z, 1 - core)
    peers = [mate]
    for axis in "xyz":
        peers += [at(axis, (here[axis] + i) % size[axis]) for i in range(1, size[axis])]
    greet(peers)

    colours, own, own_col = gather_plan(rows, x, y, z)
    local = []
    for i, (start, count, row) in enumerate(own):
        local.append(pltpu.make_async_copy(
            block_ref.at[pl.ds(start, count), :],
            embed.at[pl.ds(row, count), pl.ds(own_col, LANES)],
            local_sem.at[i],
        ))
    per = cent_ref.shape[0]
    mine, theirs = aligned(core * per, 256), aligned((1 - core) * per, 256)
    for c in range(8):
        local.append(pltpu.make_async_copy(
            cent_ref.at[:, pl.ds(c * LANES, LANES)],
            cents.at[pl.ds(mine, per), pl.ds(((c % 2) * NX + c // 2) * LANES, LANES)],
            local_sem.at[3 + c],
        ))
    for copy in local:
        copy.start()
    for copy in local:
        copy.wait()

    def view(box):
        row, count, col, width = box
        return embed.at[pl.ds(row, count), pl.ds(col, width)]

    plans = [ring_steps(stages, here, size) for stages in colours]
    slot = 0
    arriving, sent = [[] for _ in plans], []
    for t in range(len(plans[0])):
        for c, plan in enumerate(plans):
            for copy in arriving[c]:
                copy.wait_recv()
            arriving[c] = []
            for way, axis, out_boxes, in_boxes in plan[t]:
                target = at(axis, (here[axis] + way + size[axis]) % size[axis])
                for o, i in zip(out_boxes, in_boxes):
                    send = pltpu.make_async_remote_copy(
                        src_ref=view(o), dst_ref=view(o), send_sem=send_sem.at[slot],
                        recv_sem=recv_sem.at[slot], device_id=target, device_id_type=MESH)
                    send.start()
                    sent.append(send)
                    arriving[c].append(pltpu.make_async_remote_copy(
                        src_ref=view(i), dst_ref=view(i), send_sem=send_sem.at[slot],
                        recv_sem=recv_sem.at[slot], device_id=target, device_id_type=MESH))
                    slot += 1
        if t == 0:
            share = pltpu.make_async_remote_copy(
                src_ref=cents.at[pl.ds(mine, per), :], dst_ref=cents.at[pl.ds(mine, per), :],
                send_sem=cent_sem.at[0], recv_sem=cent_sem.at[1], device_id=mate, device_id_type=MESH)
            share.start()
    for copies in arriving:
        for copy in copies:
            copy.wait_recv()
    for copy in sent:
        copy.wait_send()
    share.wait_send()
    pltpu.make_async_remote_copy(
        src_ref=cents.at[pl.ds(theirs, per), :], dst_ref=cents.at[pl.ds(theirs, per), :],
        send_sem=cent_sem.at[0], recv_sem=cent_sem.at[1], device_id=mate, device_id_type=MESH).wait_recv()

    count = embed.shape[0]

    def score(i, _):
        span = pl.ds(aligned(i * chunk, chunk), chunk)
        scores = lax.dot_general(
            cents[...], embed[span, :], (((1,), (1,)), ((), ())), preferred_element_type=jnp.float32
        ) * inverse
        top = jnp.max(scores, axis=0, keepdims=True)
        powers = jnp.exp(scores - top)
        expo[:, span] = powers
        maxima[:, span] = top
        logs[:, span] = top + jnp.log(jnp.sum(powers, axis=0, keepdims=True))
        return 0

    lax.fori_loop(0, count // chunk, score, 0)

    base = 0
    for stage, axis in enumerate("xyz"):
        n, me = size[axis], here[axis]
        source = logs if stage == 0 else total.at[stage - 1]
        copies = []
        for i in range(1, n):
            copies.append(pltpu.make_async_remote_copy(
                src_ref=source, dst_ref=heard.at[base + i - 1], send_sem=lse_send.at[base + i - 1],
                recv_sem=lse_recv.at[base + i - 1], device_id=at(axis, (me + i) % n), device_id_type=MESH))
        for copy in copies:
            copy.start()
        for copy in copies:
            copy.wait_recv()
        parts = [source[...]] + [heard[base + i] for i in range(n - 1)]
        top = functools.reduce(jnp.maximum, parts)
        total[stage] = top + jnp.log(sum(jnp.exp(p - top) for p in parts))
        for copy in copies:
            copy.wait_send()
        base += n - 1
    maxima[...] = jnp.exp(maxima[...] - total[2])

    width = cents.shape[0]
    lanes = 256

    def weigh(i, tally):
        span = pl.ds(aligned(i * chunk, chunk), chunk)
        p = expo[:, span] * maxima[:, span]
        prob[:, span] = p.astype(jnp.bfloat16)
        return tally + sum(p[:, j * LANES:(j + 1) * LANES] for j in range(chunk // LANES))

    tally = lax.fori_loop(0, count // chunk, weigh, jnp.zeros((width, LANES), jnp.float32))
    tally = scale_up * jnp.sum(tally.T, axis=0, keepdims=True)
    sent_count[...] = tally

    def product(start, j):
        return scale_up * lax.dot_general(
            prob[pl.ds(start, per), :], embed[:, j * lanes:(j + 1) * lanes],
            (((1,), (0,)), ((), ())), preferred_element_type=jnp.float32)

    give = []
    for j in range(embed.shape[1] // lanes):
        cols = pl.ds(j * lanes, lanes)
        own_sum[:, cols] = product(theirs, j)
        give.append(pltpu.make_async_remote_copy(
            src_ref=own_sum.at[:, cols], dst_ref=other_sum.at[:, cols], send_sem=out_sem.at[0, j],
            recv_sem=out_sem.at[1, j], device_id=mate, device_id_type=MESH))
        give[-1].start()
    give.append(pltpu.make_async_remote_copy(
        src_ref=sent_count, dst_ref=other_count, send_sem=out_sem.at[0, 4],
        recv_sem=out_sem.at[1, 4], device_id=mate, device_id_type=MESH))
    give[-1].start()
    for j in range(embed.shape[1] // lanes):
        part = product(mine, j)
        give[j].wait_recv()
        part = part + other_sum[:, j * lanes:(j + 1) * lanes]
        for b in range(lanes // LANES):
            q = j * (lanes // LANES) + b
            c = (q % NX) * 2 + q // NX
            weighted_ref[:, c * LANES:(c + 1) * LANES] = part[:, b * LANES:(b + 1) * LANES]
    give[-1].wait_recv()
    counts_ref[...] = sent_count[:, pl.ds(mine, per)] + other_count[:, pl.ds(mine, per)]
    for copy in give:
        copy.wait_send()


def cluster(block, centroids, passages):
    per, embed_width = centroids.shape
    centres = per * lax.axis_size("dp") * lax.axis_size("cent")
    part = block.shape[0]
    r2 = part // 3 // 16 * 16
    r0 = (part - r2) // 2
    rows = (r0, part - r2 - r0, r2)
    count = passages // 2
    vmem = pl.BlockSpec(memory_space=pltpu.VMEM)
    hbm = pl.BlockSpec(memory_space=pl.ANY)
    slots = 16 + 20 + 20
    weighted, counts = pl.pallas_call(
        functools.partial(main_kernel, rows, 256, 1.0 / (math.sqrt(embed_width) * 0.05), centres / passages),
        out_shape=(
            jax.ShapeDtypeStruct((per, embed_width), jnp.float32),
            jax.ShapeDtypeStruct((1, per), jnp.float32),
        ),
        in_specs=[hbm, hbm],
        out_specs=(vmem, vmem),
        scratch_shapes=[
            pltpu.VMEM((count, embed_width), jnp.bfloat16),
            pltpu.VMEM((2 * per, embed_width), jnp.bfloat16),
            pltpu.VMEM((2 * per, count), jnp.float32),
            pltpu.VMEM((2 * per, count), jnp.bfloat16),
            pltpu.VMEM((1, count), jnp.float32),
            pltpu.VMEM((1, count), jnp.float32),
            pltpu.VMEM((3, 1, count), jnp.float32),
            pltpu.VMEM((NX + NY + NZ - 3, 1, count), jnp.float32),
            pltpu.VMEM((per, embed_width), jnp.float32),
            pltpu.VMEM((per, embed_width), jnp.float32),
            pltpu.VMEM((1, 2 * per), jnp.float32),
            pltpu.VMEM((1, 2 * per), jnp.float32),
            pltpu.SemaphoreType.DMA((slots,)),
            pltpu.SemaphoreType.DMA((slots,)),
            pltpu.SemaphoreType.DMA((11,)),
            pltpu.SemaphoreType.DMA((2,)),
            pltpu.SemaphoreType.DMA((NX + NY + NZ - 3,)),
            pltpu.SemaphoreType.DMA((NX + NY + NZ - 3,)),
            pltpu.SemaphoreType.DMA((2, 5)),
        ],
        compiler_params=pltpu.CompilerParams(
            collective_id=0, has_side_effects=True, vmem_limit_bytes=60 * 1024 * 1024),
        name="cluster",
    )(block, centroids)
    return weighted, counts.reshape(per)


def body(hidden, residual, down_weight, gain, proj_weight, centroids):
    partial_layer = jnp.dot(
        hidden,
        lax.all_gather(down_weight, "dp", axis=1, tiled=True),
        preferred_element_type=jnp.float32,
    )
    layer_out = lax.psum_scatter(partial_layer, "cent", scatter_dimension=1, tiled=True)
    normed = ((layer_out + residual.astype(jnp.float32)) * gain).astype(jnp.bfloat16)
    partial_embed = jnp.dot(normed, proj_weight, preferred_element_type=jnp.float32)
    embed_full = lax.psum(partial_embed, "cent")
    scaled = (
        embed_full * lax.rsqrt(jnp.mean(embed_full * embed_full, axis=1, keepdims=True) + 1e-06)
    ).astype(jnp.bfloat16)
    block = lax.dynamic_slice_in_dim(scaled, lax.axis_index("cent") * LANES, LANES, axis=1)
    return cluster(block, centroids, hidden.shape[0] * lax.axis_size("dp"))


def solution(mesh):
    in_specs = (
        P("dp", "cent"),
        P("dp", "cent"),
        P("cent", "dp"),
        P("cent"),
        P("cent", None),
        P(("dp", "cent"), None),
    )
    out_specs = (P(("dp", "cent"), None), P(("dp", "cent")))
    return jax.shard_map(body, mesh=mesh, in_specs=in_specs, out_specs=out_specs, check_vma=False)
```

```python
import functools
import math

import jax
import jax.numpy as jnp
from jax import lax
from jax.experimental import pallas as pl
from jax.experimental.pallas import tpu as pltpu
from jax.sharding import PartitionSpec as P

MESH = pl.DeviceIdType.MESH
NX, NY, NZ = 4, 4, 8
NL = 4
LANES = 128


def coordinates():
    dp, cent = lax.axis_index("dp"), lax.axis_index("cent")
    y, low, core = dp // (2 * NL), (dp // 2) % NL, dp % 2
    return cent // 2, y, (cent % 2) * NL + low, core


def device(x, y, z, core):
    return (y * (2 * NL) + (z % NL) * 2 + core, x * 2 + z // NL)


def aligned(value, multiple):
    return pl.multiple_of(value, multiple)


def greet(peers):
    barrier = pltpu.get_barrier_semaphore()
    for peer in peers:
        pl.semaphore_signal(barrier, inc=1, device_id=peer, device_id_type=MESH)
    pl.semaphore_wait(barrier, len(peers))


def gather_plan(rows, x, y, z):
    low, high = z % NL, z // NL
    r0, r1, r2 = rows
    b0, b1, b2 = 0, 16 * r0, 16 * (r0 + r1)

    def box(row, count, col, width):
        return (aligned(row, 16), count, aligned(col, LANES), width)

    def column(zc, xc):
        return ((zc // NL) * NX + xc) * LANES

    first = (
        ("x", lambda i: [box(b0 + (low * NY + y) * r0, r0, (high * NX + i) * LANES, LANES)]),
        ("y", lambda i: [box(b0 + (low * NY + i) * r0, r0, high * NX * LANES, NX * LANES)]),
        ("z", lambda i: [box(b0 + (i % NL) * NY * r0, NY * r0, (i // NL) * NX * LANES, NX * LANES)]),
    )
    second = (
        ("y", lambda i: [box(b1 + (low * NY + i) * r1, r1, column(z, x), LANES)]),
        ("z", lambda i: [box(b1 + (i % NL) * NY * r1, NY * r1, column(i, x), LANES)]),
        ("x", lambda i: [box(b1, 16 * r1, (h * NX + i) * LANES, LANES) for h in range(2)]),
    )
    third = (
        ("z", lambda i: [box(b2 + (y * NL + i % NL) * r2, r2, column(i, x), LANES)]),
        ("x", lambda i: [box(b2 + y * NL * r2, NL * r2, (h * NX + i) * LANES, LANES) for h in range(2)]),
        ("y", lambda i: [box(b2 + i * NL * r2, NL * r2, 0, 2 * NX * LANES)]),
    )
    own = (
        (0, r0, aligned(b0 + (low * NY + y) * r0, 16)),
        (r0, r1, aligned(b1 + (low * NY + y) * r1, 16)),
        (r0 + r1, r2, aligned(b2 + (y * NL + low) * r2, 16)),
    )
    return (first, second, third), own, aligned(column(z, x), LANES)


def half(box, which):
    row, count, col, width = box
    upper = (count // 2 + 15) // 16 * 16
    return (row, upper, col, width) if which == 0 else (aligned(row + upper, 16), count - upper, col, width)


def ring_steps(stages, position, size):
    steps = []
    for axis, boxes in stages:
        n, me = size[axis], position[axis]
        for s in range(1, n // 2 + 1):
            sends = []
            for which, way in ((0, 1), (1, -1)):
                sent = boxes((me - way * (s - 1) + n) % n)
                got = boxes((me - way * s + n) % n)
                if s == n // 2:
                    sent, got = [half(b, which) for b in sent], [half(b, which) for b in got]
                sends.append((way, axis, sent, got))
            steps.append(sends)
    return steps


def main_kernel(
    rows, chunk, inverse, scale_up,
    block_ref, cent_ref, weighted_ref, counts_ref,
    embed, cents, expo, prob, maxima, logs, total, heard, other_sum, own_sum, other_count, sent_count,
    send_sem, recv_sem, local_sem, cent_sem, lse_send, lse_recv, out_sem,
):
    x, y, z, core = coordinates()
    here = {"x": x, "y": y, "z": z}
    size = {"x": NX, "y": NY, "z": NZ}

    def at(axis, value):
        place = dict(here)
        place[axis] = value
        return device(place["x"], place["y"], place["z"], core)

    mate = device(x, y, z, 1 - core)
    peers = [mate]
    for axis in "xyz":
        peers += [at(axis, (here[axis] + i) % size[axis]) for i in range(1, size[axis])]
    greet(peers)

    colours, own, own_col = gather_plan(rows, x, y, z)
    local = []
    for i, (start, count, row) in enumerate(own):
        local.append(pltpu.make_async_copy(
            block_ref.at[pl.ds(start, count), :],
            embed.at[pl.ds(row, count), pl.ds(own_col, LANES)],
            local_sem.at[i],
        ))
    per = cent_ref.shape[0]
    mine, theirs = aligned(core * per, 256), aligned((1 - core) * per, 256)
    for c in range(8):
        local.append(pltpu.make_async_copy(
            cent_ref.at[:, pl.ds(c * LANES, LANES)],
            cents.at[pl.ds(mine, per), pl.ds(((c % 2) * NX + c // 2) * LANES, LANES)],
            local_sem.at[3 + c],
        ))
    for copy in local:
        copy.start()
    for copy in local:
        copy.wait()

    def view(box):
        row, count, col, width = box
        return embed.at[pl.ds(row, count), pl.ds(col, width)]

    plans = [ring_steps(stages, here, size) for stages in colours]
    slot = 0
    arriving, sent = [[] for _ in plans], []
    for t in range(len(plans[0])):
        for c, plan in enumerate(plans):
            for copy in arriving[c]:
                copy.wait_recv()
            arriving[c] = []
            for way, axis, out_boxes, in_boxes in plan[t]:
                target = at(axis, (here[axis] + way + size[axis]) % size[axis])
                for o, i in zip(out_boxes, in_boxes):
                    send = pltpu.make_async_remote_copy(
                        src_ref=view(o), dst_ref=view(o), send_sem=send_sem.at[slot],
                        recv_sem=recv_sem.at[slot], device_id=target, device_id_type=MESH)
                    send.start()
                    sent.append(send)
                    arriving[c].append(pltpu.make_async_remote_copy(
                        src_ref=view(i), dst_ref=view(i), send_sem=send_sem.at[slot],
                        recv_sem=recv_sem.at[slot], device_id=target, device_id_type=MESH))
                    slot += 1
        if t == 0:
            share = pltpu.make_async_remote_copy(
                src_ref=cents.at[pl.ds(mine, per), :], dst_ref=cents.at[pl.ds(mine, per), :],
                send_sem=cent_sem.at[0], recv_sem=cent_sem.at[1], device_id=mate, device_id_type=MESH)
            share.start()
    for copies in arriving:
        for copy in copies:
            copy.wait_recv()
    for copy in sent:
        copy.wait_send()
    share.wait_send()
    pltpu.make_async_remote_copy(
        src_ref=cents.at[pl.ds(theirs, per), :], dst_ref=cents.at[pl.ds(theirs, per), :],
        send_sem=cent_sem.at[0], recv_sem=cent_sem.at[1], device_id=mate, device_id_type=MESH).wait_recv()

    count = embed.shape[0]

    def score(i, _):
        span = pl.ds(aligned(i * chunk, chunk), chunk)
        scores = lax.dot_general(
            cents[...], embed[span, :], (((1,), (1,)), ((), ())), preferred_element_type=jnp.float32
        ) * inverse
        top = jnp.max(scores, axis=0, keepdims=True)
        powers = jnp.exp(scores - top)
        expo[:, span] = powers
        maxima[:, span] = top
        logs[:, span] = top + jnp.log(jnp.sum(powers, axis=0, keepdims=True))
        return 0

    lax.fori_loop(0, count // chunk, score, 0)

    base = 0
    for stage, axis in enumerate("xyz"):
        n, me = size[axis], here[axis]
        source = logs if stage == 0 else total.at[stage - 1]
        copies = []
        for i in range(1, n):
            copies.append(pltpu.make_async_remote_copy(
                src_ref=source, dst_ref=heard.at[base + i - 1], send_sem=lse_send.at[base + i - 1],
                recv_sem=lse_recv.at[base + i - 1], device_id=at(axis, (me + i) % n), device_id_type=MESH))
        for copy in copies:
            copy.start()
        for copy in copies:
            copy.wait_recv()
        parts = [source[...]] + [heard[base + i] for i in range(n - 1)]
        top = functools.reduce(jnp.maximum, parts)
        total[stage] = top + jnp.log(sum(jnp.exp(p - top) for p in parts))
        for copy in copies:
            copy.wait_send()
        base += n - 1
    maxima[...] = jnp.exp(maxima[...] - total[2])

    width = cents.shape[0]
    lanes = 256

    def weigh(i, tally):
        span = pl.ds(aligned(i * chunk, chunk), chunk)
        p = expo[:, span] * maxima[:, span]
        prob[:, span] = p.astype(jnp.bfloat16)
        return tally + sum(p[:, j * LANES:(j + 1) * LANES] for j in range(chunk // LANES))

    tally = lax.fori_loop(0, count // chunk, weigh, jnp.zeros((width, LANES), jnp.float32))
    tally = scale_up * jnp.sum(tally.T, axis=0, keepdims=True)
    sent_count[...] = tally

    def product(start, j):
        return scale_up * lax.dot_general(
            prob[pl.ds(start, per), :], embed[:, j * lanes:(j + 1) * lanes],
            (((1,), (0,)), ((), ())), preferred_element_type=jnp.float32)

    give = []
    for j in range(embed.shape[1] // lanes):
        cols = pl.ds(j * lanes, lanes)
        own_sum[:, cols] = product(theirs, j)
        give.append(pltpu.make_async_remote_copy(
            src_ref=own_sum.at[:, cols], dst_ref=other_sum.at[:, cols], send_sem=out_sem.at[0, j],
            recv_sem=out_sem.at[1, j], device_id=mate, device_id_type=MESH))
        give[-1].start()
    give.append(pltpu.make_async_remote_copy(
        src_ref=sent_count, dst_ref=other_count, send_sem=out_sem.at[0, 4],
        recv_sem=out_sem.at[1, 4], device_id=mate, device_id_type=MESH))
    give[-1].start()
    for j in range(embed.shape[1] // lanes):
        part = product(mine, j)
        give[j].wait_recv()
        part = part + other_sum[:, j * lanes:(j + 1) * lanes]
        for b in range(lanes // LANES):
            q = j * (lanes // LANES) + b
            c = (q % NX) * 2 + q // NX
            weighted_ref[:, c * LANES:(c + 1) * LANES] = part[:, b * LANES:(b + 1) * LANES]
    give[-1].wait_recv()
    counts_ref[...] = sent_count[:, pl.ds(mine, per)] + other_count[:, pl.ds(mine, per)]
    for copy in give:
        copy.wait_send()


def cluster(block, centroids, passages):
    per, embed_width = centroids.shape
    centres = per * lax.axis_size("dp") * lax.axis_size("cent")
    part = block.shape[0]
    r2 = part // 3 // 16 * 16
    r0 = (part - r2) // 2
    rows = (r0, part - r2 - r0, r2)
    count = passages // 2
    vmem = pl.BlockSpec(memory_space=pltpu.VMEM)
    hbm = pl.BlockSpec(memory_space=pl.ANY)
    slots = 16 + 20 + 20
    weighted, counts = pl.pallas_call(
        functools.partial(main_kernel, rows, 256, 1.0 / (math.sqrt(embed_width) * 0.05), centres / passages),
        out_shape=(
            jax.ShapeDtypeStruct((per, embed_width), jnp.float32),
            jax.ShapeDtypeStruct((1, per), jnp.float32),
        ),
        in_specs=[hbm, hbm],
        out_specs=(vmem, vmem),
        scratch_shapes=[
            pltpu.VMEM((count, embed_width), jnp.bfloat16),
            pltpu.VMEM((2 * per, embed_width), jnp.bfloat16),
            pltpu.VMEM((2 * per, count), jnp.float32),
            pltpu.VMEM((2 * per, count), jnp.bfloat16),
            pltpu.VMEM((1, count), jnp.float32),
            pltpu.VMEM((1, count), jnp.float32),
            pltpu.VMEM((3, 1, count), jnp.float32),
            pltpu.VMEM((NX + NY + NZ - 3, 1, count), jnp.float32),
            pltpu.VMEM((per, embed_width), jnp.float32),
            pltpu.VMEM((per, embed_width), jnp.float32),
            pltpu.VMEM((1, 2 * per), jnp.float32),
            pltpu.VMEM((1, 2 * per), jnp.float32),
            pltpu.SemaphoreType.DMA((slots,)),
            pltpu.SemaphoreType.DMA((slots,)),
            pltpu.SemaphoreType.DMA((11,)),
            pltpu.SemaphoreType.DMA((2,)),
            pltpu.SemaphoreType.DMA((NX + NY + NZ - 3,)),
            pltpu.SemaphoreType.DMA((NX + NY + NZ - 3,)),
            pltpu.SemaphoreType.DMA((2, 5)),
        ],
        compiler_params=pltpu.CompilerParams(
            collective_id=0, has_side_effects=True, vmem_limit_bytes=60 * 1024 * 1024),
        name="cluster",
    )(block, centroids)
    return weighted, counts.reshape(per)


def encode_kernel(
    hidden_ref, residual_ref, down_ref, gain_ref, proj_ref, block_ref,
    down, hid, res, layer, heard_l, sums_l, heard_f, mix, heard_m, sums_x, heard_x, sums_h, heard_h, square, squares,
    send_sem, recv_sem, local_sem, unit_send, unit_recv,
):
    x, y, z, core = coordinates()
    low, high = z % NL, z // NL
    mate = device(x, y, z, 1 - core)
    far = device(x, y, (z + NL) % NZ, core)

    def at_x(i):
        return device((x + i) % NX, y, z, core)

    def at_far(i):
        return device((x + i) % NX, y, (z + NL) % NZ, core)

    def at_y(i):
        return device(x, (y + i) % NY, z, core)

    def at_low(i):
        return device(x, y, high * NL + (low + i) % NL, core)

    greet([mate, far, at_y(1), at_y(3)] + [f(i) for f in (at_x, at_far, at_low) for i in (1, 2, 3)])

    used, done = [0], []

    def remote(src, dst, target):
        i = used[0]
        used[0] += 1
        copy = pltpu.make_async_remote_copy(
            src_ref=src, dst_ref=dst, send_sem=send_sem.at[i], recv_sem=recv_sem.at[i],
            device_id=target, device_id_type=MESH)
        copy.start()
        done.append(copy)
        return copy

    kept = []

    def local(src, dst):
        copy = pltpu.make_async_copy(src, dst, local_sem.at[len(kept)])
        copy.start()
        kept.append(copy)

    units, width = down_ref.shape
    passages = hidden_ref.shape[0]
    pair = 2 * LANES

    def tile(yc, zc, start=0, count=units):
        return down.at[yc, zc // 2, pl.ds(start, count), pl.ds(aligned((zc % 2) * LANES, LANES), LANES)]

    along_z = {i: remote(down_ref, tile(y, low), at_low(i)) for i in (1, 3, 2)}
    ring = {0: (remote(down_ref, tile(y, low), at_y(1)), remote(down_ref, tile(y, low), at_y(3)))}
    local(down_ref, tile(y, low))

    rows = pl.ds(aligned(core * passages, 16), passages)
    mates = pl.ds(aligned((1 - core) * passages, 16), passages)
    from_mate = [remote(hidden_ref, hid.at[rows, :], mate)]
    local(hidden_ref, hid.at[rows, :])
    for b in range(2):
        to = pl.ds(b * LANES, LANES)
        col = aligned(b * pair + (1 - core) * LANES, LANES)
        from_mate.append(remote(residual_ref.at[:, pl.ds(col, LANES)], res.at[rows, to], mate))
        col = aligned(b * pair + core * LANES, LANES)
        local(residual_ref.at[:, pl.ds(col, LANES)], res.at[rows, to])

    cut = units // 32 * 16

    def relay(zi):
        zc = (low - zi + NL) % NL
        for copy in ring[zi]:
            copy.wait_recv()
        lower = tile((y + 3) % NY, zc, 0, cut)
        upper = tile((y + 1) % NY, zc, cut, units - cut)
        return remote(lower, lower, at_y(1)), remote(upper, upper, at_y(3))

    order = (0, 1, 3, 2)
    relays = []
    for n, zi in enumerate(order):
        if n:
            zc = (low - zi + NL) % NL
            along_z[zi].wait_recv()
            ring[zi] = (remote(tile(y, zc), tile(y, zc), at_y(1)), remote(tile(y, zc), tile(y, zc), at_y(3)))
            relays += relay(order[n - 1])
    for copy in kept:
        copy.wait()
    for copy in from_mate:
        copy.wait_recv()

    sent_units = []

    def unit(o):
        yc = (y + o) % NY
        for h in range(2):
            layer[yc, h] = jnp.dot(hid[...], down[yc, h], preferred_element_type=jnp.float32)
        step = (yc - x + NX) % NX
        slot = (step + NX - 1) % NX
        copy = pltpu.make_async_remote_copy(
            src_ref=layer.at[yc], dst_ref=heard_l.at[slot], send_sem=unit_send.at[o],
            recv_sem=unit_recv.at[slot], device_id=device(yc, y, z, core), device_id_type=MESH)

        @pl.when(step != 0)
        def _():
            copy.start()

        sent_units.append((step, copy))

    unit(0)
    relays += relay(order[-1])
    unit(1)
    unit(3)
    for copy in relays:
        copy.wait_recv()
    unit(2)

    for i in range(NX - 1):
        pltpu.make_async_remote_copy(
            src_ref=heard_l.at[i], dst_ref=heard_l.at[i], send_sem=unit_send.at[i],
            recv_sem=unit_recv.at[i], device_id=at_x(1), device_id_type=MESH).wait_recv()

    def over_x(h):
        value = layer[x, h]
        for i in range(NX - 1):
            value = value + heard_l[i, h]
        return value

    sums_l[...] = over_x(1 - high)
    other = remote(sums_l, heard_f, far)
    value = over_x(high)
    other.wait_recv()
    value = value + heard_f[...] + res[...].astype(jnp.float32)
    gain = jnp.concatenate([gain_ref[core], gain_ref[2 + core]], axis=1)
    normed = (value * gain).astype(jnp.bfloat16)
    proj = jnp.concatenate(
        [proj_ref[pl.ds(aligned(b * pair + core * LANES, LANES), LANES), :] for b in range(2)], axis=0)
    mix[...] = jnp.dot(normed, proj, preferred_element_type=jnp.float32)
    other = remote(mix.at[mates, :], heard_m, mate)
    other.wait_recv()
    wide = sums_x.shape[2]
    for q in range(NX):
        cols = pl.ds(q * wide, wide)
        sums_x[q] = mix[rows, cols] + heard_m[:, cols]
    stage = [remote(sums_x.at[(x + i) % NX], heard_x.at[i - 1], at_x(i)) for i in (1, 2, 3)]
    for copy in stage:
        copy.wait_recv()
    value = sums_x[x]
    for i in range(NX - 1):
        value = value + heard_x[i]
    for h in range(2):
        sums_h[h] = value[:, h * LANES:(h + 1) * LANES]
    remote(sums_h.at[1 - high], heard_h, far).wait_recv()
    value = sums_h[high] + heard_h[...]

    pad = square.shape[1] - passages
    squared = jnp.concatenate([value * value, jnp.zeros((pad, LANES), jnp.float32)], axis=0)
    square[...] = jnp.sum(squared.T, axis=0, keepdims=True)
    stage = [remote(square, squares.at[i - 1], at_x(i)) for i in (1, 2, 3)]
    stage += [remote(square, squares.at[3 + i], at_far(i)) for i in range(4)]
    for copy in stage:
        copy.wait_recv()
    total = square[...]
    for i in range(7):
        total = total + squares[i]
    norm = lax.rsqrt(total * (1.0 / proj_ref.shape[1]) + 1e-06)
    norm = jnp.broadcast_to(norm, (LANES, norm.shape[1])).T
    block_ref[...] = (value * norm[:passages]).astype(jnp.bfloat16)

    for step, copy in sent_units:
        @pl.when(step != 0)
        def _():
            copy.wait_send()

    for copy in done:
        copy.wait_send()


def encode(hidden, residual, down_weight, gain, proj_weight):
    passages, units = hidden.shape
    features, embed_width = proj_weight.shape
    vmem = pl.BlockSpec(memory_space=pltpu.VMEM)
    hbm = pl.BlockSpec(memory_space=pl.ANY)
    bf16, f32 = jnp.bfloat16, jnp.float32
    pair, both = 2 * LANES, 2 * passages
    padded = (passages + LANES - 1) // LANES * LANES
    slots = 3 + 8 + 8 + 3 + 1 + 1 + 3 + 1 + 7
    return pl.pallas_call(
        encode_kernel,
        out_shape=jax.ShapeDtypeStruct((passages, LANES), bf16),
        in_specs=[hbm, hbm, hbm, vmem, vmem],
        out_specs=vmem,
        scratch_shapes=[
            pltpu.VMEM((NY, 2, units, pair), bf16),
            pltpu.VMEM((both, units), bf16),
            pltpu.VMEM((both, pair), bf16),
            pltpu.VMEM((NX, 2, both, pair), f32),
            pltpu.VMEM((NX, 2, both, pair), f32),
            pltpu.VMEM((both, pair), f32),
            pltpu.VMEM((both, pair), f32),
            pltpu.VMEM((both, embed_width), f32),
            pltpu.VMEM((passages, embed_width), f32),
            pltpu.VMEM((NX, passages, pair), f32),
            pltpu.VMEM((NX - 1, passages, pair), f32),
            pltpu.VMEM((2, passages, LANES), f32),
            pltpu.VMEM((passages, LANES), f32),
            pltpu.VMEM((1, padded), f32),
            pltpu.VMEM((7, 1, padded), f32),
            pltpu.SemaphoreType.DMA((slots,)),
            pltpu.SemaphoreType.DMA((slots,)),
            pltpu.SemaphoreType.DMA((4,)),
            pltpu.SemaphoreType.DMA((NY,)),
            pltpu.SemaphoreType.DMA((NX,)),
        ],
        compiler_params=pltpu.CompilerParams(
            collective_id=1, has_side_effects=True, vmem_limit_bytes=48 * 1024 * 1024),
        name="encode",
    )(hidden, residual, down_weight, gain.reshape(features // LANES, 1, LANES), proj_weight)


def body(hidden, residual, down_weight, gain, proj_weight, centroids):
    block = encode(hidden, residual, down_weight, gain, proj_weight)
    return cluster(block, centroids, hidden.shape[0] * lax.axis_size("dp"))


def solution(mesh):
    in_specs = (
        P("dp", "cent"),
        P("dp", "cent"),
        P("cent", "dp"),
        P("cent"),
        P("cent", None),
        P(("dp", "cent"), None),
    )
    out_specs = (P(("dp", "cent"), None), P(("dp", "cent")))
    return jax.shard_map(body, mesh=mesh, in_specs=in_specs, out_specs=out_specs, check_vma=False)
```

```python
import functools
import math

import jax
import jax.numpy as jnp
from jax import lax
from jax.experimental import pallas as pl
from jax.experimental.pallas import tpu as pltpu
from jax.sharding import PartitionSpec as P

MESH = pl.DeviceIdType.MESH
NX, NY, NZ = 4, 4, 8
NL = 4
LANES = 128


def coordinates():
    dp, cent = lax.axis_index("dp"), lax.axis_index("cent")
    y, low, core = dp // (2 * NL), (dp // 2) % NL, dp % 2
    return cent // 2, y, (cent % 2) * NL + low, core


def device(x, y, z, core):
    return (y * (2 * NL) + (z % NL) * 2 + core, x * 2 + z // NL)


def aligned(value, multiple):
    return pl.multiple_of(value, multiple)


def greet(peers):
    barrier = pltpu.get_barrier_semaphore()
    for peer in peers:
        pl.semaphore_signal(barrier, inc=1, device_id=peer, device_id_type=MESH)
    pl.semaphore_wait(barrier, len(peers))


def gather_plan(rows, x, y, z):
    low, high = z % NL, z // NL
    r0, r1, r2 = rows
    b0, b1, b2 = 0, 16 * r0, 16 * (r0 + r1)

    def box(row, count, col, width):
        return (aligned(row, 16), count, aligned(col, LANES), width)

    def column(zc, xc):
        return ((zc // NL) * NX + xc) * LANES

    first = (
        ("x", 2, lambda i: [box(b0 + (low * NY + y) * r0, r0, (high * NX + i) * LANES, LANES)]),
        ("y", 2, lambda i: [box(b0 + (low * NY + i) * r0, r0, high * NX * LANES, NX * LANES)]),
        ("z", 4, lambda i: [box(b0 + (i % NL) * NY * r0, NY * r0, (i // NL) * NX * LANES, NX * LANES)]),
    )
    second = (
        ("y", 2, lambda i: [box(b1 + (low * NY + i) * r1, r1, column(z, x), LANES)]),
        ("z", 2, lambda i: [box(b1 + (i % NL) * NY * r1, NY * r1, column(i, x), LANES)]),
        ("x", 2, lambda i: [box(b1, 16 * r1, (h * NX + i) * LANES, LANES) for h in range(2)]),
    )
    third = (
        ("z", 2, lambda i: [box(b2 + (y * NL + i % NL) * r2, r2, column(i, x), LANES)]),
        ("x", 1, lambda i: [box(b2 + y * NL * r2, NL * r2, (h * NX + i) * LANES, LANES) for h in range(2)]),
        ("y", 4, lambda i: [box(b2 + i * NL * r2, NL * r2, 0, 2 * NX * LANES)]),
    )
    own = (
        (0, r0, aligned(b0 + (low * NY + y) * r0, 16)),
        (r0, r1, aligned(b1 + (low * NY + y) * r1, 16)),
        (r0 + r1, r2, aligned(b2 + (y * NL + low) * r2, 16)),
    )
    return (first, second, third), own, aligned(column(z, x), LANES)


def pieces(boxes, cuts):
    out = []
    for row, count, col, width in boxes:
        start = 0
        for left in range(cuts, 0, -1):
            size = ((count - start) // 16 + left - 1) // left * 16
            out.append((aligned(row + start, 16), size, col, width))
            start += size
    return out


def ring_sends(plans, position, size):
    sends, free = [], {}
    hop, rate = 1.7, 45.0e3
    for colour, stages in enumerate(plans):
        before = []
        for axis, cuts, boxes in stages:
            n, me = size[axis], position[axis]
            now, chain = [], {}
            for s in range(1, n // 2 + 1):
                for way in (1, -1):
                    out = pieces(boxes((me - way * (s - 1) + n) % n), cuts)
                    got = pieces(boxes((me - way * s + n) % n), cuts)
                    middle = len(out) // 2
                    keep = range(len(out))
                    if s == n // 2:
                        keep = keep[:middle] if way == 1 else keep[middle:]
                    for p in keep:
                        needs = before if s == 1 else [chain[way, s - 1, p]]
                        chain[way, s, p] = len(sends)
                        now.append(len(sends))
                        sends.append((colour, axis, way, out[p], got[p], needs))
            before = now
    order, left, arrive = [], set(range(len(sends))), {}
    while left:
        best = None
        for i in left:
            needs = sends[i][5]
            if all(n in arrive for n in needs):
                start = max([arrive[n] for n in needs] + [0.0])
                key = (max(start, free.get(sends[i][1:3], 0.0)), start, i)
                if best is None or key < best:
                    best = key
        at, start, i = best
        left.remove(i)
        _, count, _, width = sends[i][3]
        free[sends[i][1:3]] = at + count * width * 2 / rate
        arrive[i] = at + count * width * 2 / rate + hop
        order.append((start, i))
    order.sort()
    return sends, [i for _, i in order]


def main_kernel(
    rows, chunk, inverse, scale_up,
    block_ref, cent_ref, weighted_ref, counts_ref,
    embed, cents, expo, prob, maxima, logs, total, heard, other_sum, own_sum, other_count, sent_count,
    send_sem, recv_sem, local_sem, cent_sem, lse_send, lse_recv, out_sem,
):
    x, y, z, core = coordinates()
    here = {"x": x, "y": y, "z": z}
    size = {"x": NX, "y": NY, "z": NZ}

    def at(axis, value):
        place = dict(here)
        place[axis] = value
        return device(place["x"], place["y"], place["z"], core)

    mate = device(x, y, z, 1 - core)
    peers = [mate]
    for axis in "xyz":
        peers += [at(axis, (here[axis] + i) % size[axis]) for i in range(1, size[axis])]
    greet(peers)

    colours, own, own_col = gather_plan(rows, x, y, z)
    local = []
    for i, (start, count, row) in enumerate(own):
        local.append(pltpu.make_async_copy(
            block_ref.at[pl.ds(start, count), :],
            embed.at[pl.ds(row, count), pl.ds(own_col, LANES)],
            local_sem.at[i],
        ))
    per = cent_ref.shape[0]
    mine, theirs = aligned(core * per, 256), aligned((1 - core) * per, 256)
    for c in range(8):
        local.append(pltpu.make_async_copy(
            cent_ref.at[:, pl.ds(c * LANES, LANES)],
            cents.at[pl.ds(mine, per), pl.ds(((c % 2) * NX + c // 2) * LANES, LANES)],
            local_sem.at[3 + c],
        ))
    for copy in local:
        copy.start()
    for copy in local:
        copy.wait()

    def view(box):
        row, count, col, width = box
        return embed.at[pl.ds(row, count), pl.ds(col, width)]

    share = pltpu.make_async_remote_copy(
        src_ref=cents.at[pl.ds(mine, per), :], dst_ref=cents.at[pl.ds(mine, per), :],
        send_sem=cent_sem.at[0], recv_sem=cent_sem.at[1], device_id=mate, device_id_type=MESH)
    share.start()
    sends, order = ring_sends(colours, here, size)
    arrived, sent = set(), []

    def remote(i, piece):
        _, axis, way = sends[i][:3]
        return pltpu.make_async_remote_copy(
            src_ref=view(piece), dst_ref=view(piece), send_sem=send_sem.at[i], recv_sem=recv_sem.at[i],
            device_id=at(axis, (here[axis] + way + size[axis]) % size[axis]), device_id_type=MESH)

    def hear(i):
        if i not in arrived:
            arrived.add(i)
            remote(i, sends[i][4]).wait_recv()

    for i in order:
        for need in sends[i][5]:
            hear(need)
        copy = remote(i, sends[i][3])
        copy.start()
        sent.append(copy)
    for i in order:
        hear(i)
    for copy in sent:
        copy.wait_send()
    share.wait_send()
    pltpu.make_async_remote_copy(
        src_ref=cents.at[pl.ds(theirs, per), :], dst_ref=cents.at[pl.ds(theirs, per), :],
        send_sem=cent_sem.at[0], recv_sem=cent_sem.at[1], device_id=mate, device_id_type=MESH).wait_recv()

    count = embed.shape[0]

    def score(i, _):
        span = pl.ds(aligned(i * chunk, chunk), chunk)
        scores = lax.dot_general(
            cents[...], embed[span, :], (((1,), (1,)), ((), ())), preferred_element_type=jnp.float32
        ) * inverse
        top = jnp.max(scores, axis=0, keepdims=True)
        powers = jnp.exp(scores - top)
        expo[:, span] = powers
        maxima[:, span] = top
        logs[:, span] = top + jnp.log(jnp.sum(powers, axis=0, keepdims=True))
        return 0

    lax.fori_loop(0, count // chunk, score, 0)

    base = 0
    for stage, axis in enumerate("xyz"):
        n, me = size[axis], here[axis]
        source = logs if stage == 0 else total.at[stage - 1]
        copies = []
        for i in range(1, n):
            copies.append(pltpu.make_async_remote_copy(
                src_ref=source, dst_ref=heard.at[base + i - 1], send_sem=lse_send.at[base + i - 1],
                recv_sem=lse_recv.at[base + i - 1], device_id=at(axis, (me + i) % n), device_id_type=MESH))
        for copy in copies:
            copy.start()
        for copy in copies:
            copy.wait_recv()
        parts = [source[...]] + [heard[base + i] for i in range(n - 1)]
        top = functools.reduce(jnp.maximum, parts)
        total[stage] = top + jnp.log(sum(jnp.exp(p - top) for p in parts))
        for copy in copies:
            copy.wait_send()
        base += n - 1
    maxima[...] = jnp.exp(maxima[...] - total[2])

    width = cents.shape[0]
    lanes = 256

    def weigh(i, tally):
        span = pl.ds(aligned(i * chunk, chunk), chunk)
        p = expo[:, span] * maxima[:, span]
        prob[:, span] = p.astype(jnp.bfloat16)
        return tally + sum(p[:, j * LANES:(j + 1) * LANES] for j in range(chunk // LANES))

    tally = lax.fori_loop(0, count // chunk, weigh, jnp.zeros((width, LANES), jnp.float32))
    tally = scale_up * jnp.sum(tally.T, axis=0, keepdims=True)
    sent_count[...] = tally

    def product(start, j):
        return scale_up * lax.dot_general(
            prob[pl.ds(start, per), :], embed[:, j * lanes:(j + 1) * lanes],
            (((1,), (0,)), ((), ())), preferred_element_type=jnp.float32)

    give = []
    for j in range(embed.shape[1] // lanes):
        cols = pl.ds(j * lanes, lanes)
        own_sum[:, cols] = product(theirs, j)
        give.append(pltpu.make_async_remote_copy(
            src_ref=own_sum.at[:, cols], dst_ref=other_sum.at[:, cols], send_sem=out_sem.at[0, j],
            recv_sem=out_sem.at[1, j], device_id=mate, device_id_type=MESH))
        give[-1].start()
    give.append(pltpu.make_async_remote_copy(
        src_ref=sent_count, dst_ref=other_count, send_sem=out_sem.at[0, 4],
        recv_sem=out_sem.at[1, 4], device_id=mate, device_id_type=MESH))
    give[-1].start()
    for j in range(embed.shape[1] // lanes):
        part = product(mine, j)
        give[j].wait_recv()
        part = part + other_sum[:, j * lanes:(j + 1) * lanes]
        for b in range(lanes // LANES):
            q = j * (lanes // LANES) + b
            c = (q % NX) * 2 + q // NX
            weighted_ref[:, c * LANES:(c + 1) * LANES] = part[:, b * LANES:(b + 1) * LANES]
    give[-1].wait_recv()
    counts_ref[...] = sent_count[:, pl.ds(mine, per)] + other_count[:, pl.ds(mine, per)]
    for copy in give:
        copy.wait_send()


def cluster(block, centroids, passages):
    per, embed_width = centroids.shape
    centres = per * lax.axis_size("dp") * lax.axis_size("cent")
    part = block.shape[0]
    r0 = part // 3 // 16 * 16
    r1 = (part - r0) // 32 * 16
    rows = (r0, r1, part - r0 - r1)
    count = passages // 2
    vmem = pl.BlockSpec(memory_space=pltpu.VMEM)
    hbm = pl.BlockSpec(memory_space=pl.ANY)
    slots = 128
    weighted, counts = pl.pallas_call(
        functools.partial(main_kernel, rows, 256, 1.0 / (math.sqrt(embed_width) * 0.05), centres / passages),
        out_shape=(
            jax.ShapeDtypeStruct((per, embed_width), jnp.float32),
            jax.ShapeDtypeStruct((1, per), jnp.float32),
        ),
        in_specs=[hbm, hbm],
        out_specs=(vmem, vmem),
        scratch_shapes=[
            pltpu.VMEM((count, embed_width), jnp.bfloat16),
            pltpu.VMEM((2 * per, embed_width), jnp.bfloat16),
            pltpu.VMEM((2 * per, count), jnp.float32),
            pltpu.VMEM((2 * per, count), jnp.bfloat16),
            pltpu.VMEM((1, count), jnp.float32),
            pltpu.VMEM((1, count), jnp.float32),
            pltpu.VMEM((3, 1, count), jnp.float32),
            pltpu.VMEM((NX + NY + NZ - 3, 1, count), jnp.float32),
            pltpu.VMEM((per, embed_width), jnp.float32),
            pltpu.VMEM((per, embed_width), jnp.float32),
            pltpu.VMEM((1, 2 * per), jnp.float32),
            pltpu.VMEM((1, 2 * per), jnp.float32),
            pltpu.SemaphoreType.DMA((slots,)),
            pltpu.SemaphoreType.DMA((slots,)),
            pltpu.SemaphoreType.DMA((11,)),
            pltpu.SemaphoreType.DMA((2,)),
            pltpu.SemaphoreType.DMA((NX + NY + NZ - 3,)),
            pltpu.SemaphoreType.DMA((NX + NY + NZ - 3,)),
            pltpu.SemaphoreType.DMA((2, 5)),
        ],
        compiler_params=pltpu.CompilerParams(
            collective_id=0, has_side_effects=True, vmem_limit_bytes=60 * 1024 * 1024),
        name="cluster",
    )(block, centroids)
    return weighted, counts.reshape(per)


def encode_kernel(
    hidden_ref, residual_ref, down_ref, gain_ref, proj_ref, block_ref,
    down, hid, res, scale, proj, part, heard, given, heard_f, normed, turned,
    sums_x, heard_x, sums_h, heard_h, square, squares,
    send_sem, recv_sem, local_sem, part_send, part_recv,
):
    x, y, z, core = coordinates()
    low, high = z % NL, z // NL
    mate = device(x, y, z, 1 - core)
    far = device(x, y, (z + NL) % NZ, core)
    turn = device(y, x, z, core)
    alone = x == y

    def at_x(i):
        return device((x + i) % NX, y, z, core)

    def at_far(i):
        return device((x + i) % NX, y, (z + NL) % NZ, core)

    def at_y(i):
        return device(x, (y + i) % NY, z, core)

    def at_low(i):
        return device(x, y, high * NL + (low + i) % NL, core)

    peers = [mate, far] + [f(i) for f in (at_x, at_far, at_y, at_low) for i in (1, 2, 3)]
    barrier = pltpu.get_barrier_semaphore()
    for peer in peers:
        pl.semaphore_signal(barrier, inc=1, device_id=peer, device_id_type=MESH)

    @pl.when(jnp.logical_not(alone))
    def _():
        pl.semaphore_signal(barrier, inc=1, device_id=turn, device_id_type=MESH)

    pl.semaphore_wait(barrier, jnp.where(alone, len(peers), len(peers) + 1))

    used, done, kept = [0], [], []

    def remote(src, dst, target, start=True):
        i = used[0]
        used[0] += 1
        copy = pltpu.make_async_remote_copy(
            src_ref=src, dst_ref=dst, send_sem=send_sem.at[i], recv_sem=recv_sem.at[i],
            device_id=target, device_id_type=MESH)
        if start:
            copy.start()
            done.append(copy)
        return copy

    def local(src, dst, start=True):
        copy = pltpu.make_async_copy(src, dst, local_sem.at[len(kept)])
        kept.append(copy)
        if start:
            copy.start()
        return copy

    def transposed(src, dst):
        out, here = remote(src, dst, turn, False), local(src, dst, False)

        @pl.when(jnp.logical_not(alone))
        def _():
            out.start()

        @pl.when(alone)
        def _():
            here.start()

        return out, here

    def land(pair):
        @pl.when(jnp.logical_not(alone))
        def _():
            pair[0].wait()

        @pl.when(alone)
        def _():
            pair[1].wait()

    mine = pl.ds(aligned(core * LANES, LANES), LANES)
    passages = hidden_ref.shape[0]
    wide = 2 * LANES

    own = down.at[low, :, mine]
    along_z = {i: remote(down_ref, own, at_low(i)) for i in (1, 3, 2)}
    along_y = [remote(hidden_ref, hid.at[y], at_y(i)) for i in (1, 3, 2)]
    crossed = {0: remote(down_ref, own, mate)}
    first = [local(down_ref, own), local(hidden_ref, hid.at[y])]
    loaded = local(proj_ref, proj)
    moved = [transposed(residual_ref, res), transposed(gain_ref, scale)]

    for copy in along_y:
        copy.wait_recv()
    for copy in first:
        copy.wait()
    flat = (NY * passages, hid.shape[2])
    sent = []
    for zi in (0, 1, 3, 2):
        zc = (low - zi + NL) % NL
        if zi:
            along_z[zi].wait_recv()
            crossed[zi] = remote(down.at[zc, :, mine], down.at[zc, :, mine], mate)
        crossed[zi].wait_recv()
        value = jnp.dot(hid[...].reshape(flat), down[zc], preferred_element_type=jnp.float32)
        for q in range(NX):
            part[zc, q] = value[q * passages:(q + 1) * passages]
        for i in (1, 3, 2):
            copy = pltpu.make_async_remote_copy(
                src_ref=part.at[zc, (x + i) % NX], dst_ref=heard.at[zc, i - 1],
                send_sem=part_send.at[zc, i - 1], recv_sem=part_recv.at[zc, i - 1],
                device_id=at_x(i), device_id_type=MESH)
            copy.start()
            sent.append(copy)

    def over_x(zc):
        value = part[zc, x]
        for i in (1, 3, 2):
            pltpu.make_async_remote_copy(
                src_ref=heard.at[zc, i - 1], dst_ref=heard.at[zc, i - 1],
                send_sem=part_send.at[zc, i - 1], recv_sem=part_recv.at[zc, i - 1],
                device_id=at_x(i), device_id_type=MESH).wait_recv()
            value = value + heard[zc, i - 1]
        return value

    others = []
    for b in range(2):
        given[b] = over_x((1 - high) * 2 + b)
        others.append(remote(given.at[b], heard_f.at[b], far))
    for pair in moved:
        land(pair)
    for b in range(2):
        value = over_x(high * 2 + b)
        others[b].wait_recv()
        cols = pl.ds(b * wide, wide)
        gain = jnp.concatenate([scale[2 * b], scale[2 * b + 1]], axis=1)
        value = value + heard_f[b] + res[:, cols].astype(jnp.float32)
        normed[:, cols] = (value * gain).astype(jnp.bfloat16)
    land(transposed(normed, turned))
    loaded.wait()
    mixed = jnp.dot(turned[...], proj[...], preferred_element_type=jnp.float32)
    for q in range(NX):
        sums_x[q] = mixed[:, q * wide:(q + 1) * wide]
    stage = [remote(sums_x.at[(x + i) % NX], heard_x.at[i - 1], at_x(i)) for i in (1, 2, 3)]
    for copy in stage:
        copy.wait_recv()
    value = sums_x[x]
    for i in range(NX - 1):
        value = value + heard_x[i]
    for h in range(2):
        sums_h[h] = value[:, h * LANES:(h + 1) * LANES]
    remote(sums_h.at[1 - high], heard_h, far).wait_recv()
    value = sums_h[high] + heard_h[...]

    pad = square.shape[1] - passages
    squared = jnp.concatenate([value * value, jnp.zeros((pad, LANES), jnp.float32)], axis=0)
    square[...] = jnp.sum(squared.T, axis=0, keepdims=True)
    stage = [remote(square, squares.at[i - 1], at_x(i)) for i in (1, 2, 3)]
    stage += [remote(square, squares.at[3 + i], at_far(i)) for i in range(4)]
    for copy in stage:
        copy.wait_recv()
    total = square[...]
    for i in range(7):
        total = total + squares[i]
    norm = lax.rsqrt(total * (1.0 / proj_ref.shape[1]) + 1e-06)
    norm = jnp.broadcast_to(norm, (LANES, norm.shape[1])).T
    block_ref[...] = (value * norm[:passages]).astype(jnp.bfloat16)

    for copy in sent + done:
        copy.wait_send()


def encode(hidden, residual, down_weight, gain, proj_weight):
    passages, units = hidden.shape
    features, embed_width = proj_weight.shape
    vmem = pl.BlockSpec(memory_space=pltpu.VMEM)
    hbm = pl.BlockSpec(memory_space=pl.ANY)
    bf16, f32 = jnp.bfloat16, jnp.float32
    wide = 2 * LANES
    padded = (passages + LANES - 1) // LANES * LANES
    slots = 3 + 3 + 4 + 3 + 2 + 3 + 1 + 7
    return pl.pallas_call(
        encode_kernel,
        out_shape=jax.ShapeDtypeStruct((passages, LANES), bf16),
        in_specs=[hbm, hbm, hbm, hbm, hbm],
        out_specs=vmem,
        scratch_shapes=[
            pltpu.VMEM((NL, units, wide), bf16),
            pltpu.VMEM((NY, passages, units), bf16),
            pltpu.VMEM((passages, features), bf16),
            pltpu.VMEM((features // LANES, 1, LANES), f32),
            pltpu.VMEM((features, embed_width), bf16),
            pltpu.VMEM((NL, NX, passages, wide), f32),
            pltpu.VMEM((NL, NX - 1, passages, wide), f32),
            pltpu.VMEM((2, passages, wide), f32),
            pltpu.VMEM((2, passages, wide), f32),
            pltpu.VMEM((passages, features), bf16),
            pltpu.VMEM((passages, features), bf16),
            pltpu.VMEM((NX, passages, wide), f32),
            pltpu.VMEM((NX - 1, passages, wide), f32),
            pltpu.VMEM((2, passages, LANES), f32),
            pltpu.VMEM((passages, LANES), f32),
            pltpu.VMEM((1, padded), f32),
            pltpu.VMEM((7, 1, padded), f32),
            pltpu.SemaphoreType.DMA((slots,)),
            pltpu.SemaphoreType.DMA((slots,)),
            pltpu.SemaphoreType.DMA((6,)),
            pltpu.SemaphoreType.DMA((NL, NX - 1)),
            pltpu.SemaphoreType.DMA((NL, NX - 1)),
        ],
        compiler_params=pltpu.CompilerParams(
            collective_id=1, has_side_effects=True, vmem_limit_bytes=63 * 1024 * 1024),
        name="encode",
    )(hidden, residual, down_weight, gain.reshape(features // LANES, 1, LANES), proj_weight)


def body(hidden, residual, down_weight, gain, proj_weight, centroids):
    block = encode(hidden, residual, down_weight, gain, proj_weight)
    return cluster(block, centroids, hidden.shape[0] * lax.axis_size("dp"))


def solution(mesh):
    in_specs = (
        P("dp", "cent"),
        P("dp", "cent"),
        P("cent", "dp"),
        P("cent"),
        P("cent", None),
        P(("dp", "cent"), None),
    )
    out_specs = (P(("dp", "cent"), None), P(("dp", "cent")))
    return jax.shard_map(body, mesh=mesh, in_specs=in_specs, out_specs=out_specs, check_vma=False)
```

```python
import functools
import math

import jax
import jax.numpy as jnp
from jax import lax
from jax.experimental import pallas as pl
from jax.experimental.pallas import tpu as pltpu
from jax.sharding import PartitionSpec as P

MESH = pl.DeviceIdType.MESH
NX, NY, NZ = 4, 4, 8
NL = 4
LANES = 128


def coordinates():
    dp, cent = lax.axis_index("dp"), lax.axis_index("cent")
    y, low, core = dp // (2 * NL), (dp // 2) % NL, dp % 2
    return cent // 2, y, (cent % 2) * NL + low, core


def device(x, y, z, core):
    return (y * (2 * NL) + (z % NL) * 2 + core, x * 2 + z // NL)


def aligned(value, multiple):
    return pl.multiple_of(value, multiple)


def greet(peers):
    barrier = pltpu.get_barrier_semaphore()
    for peer in peers:
        pl.semaphore_signal(barrier, inc=1, device_id=peer, device_id_type=MESH)
    pl.semaphore_wait(barrier, len(peers))


def gather_plan(rows, x, y, z):
    low, high = z % NL, z // NL
    r0, r1, r2 = rows
    b0, b1, b2 = 0, 16 * r0, 16 * (r0 + r1)

    def box(row, count, col, width):
        return (aligned(row, 16), count, aligned(col, LANES), width)

    def column(zc, xc):
        return ((zc // NL) * NX + xc) * LANES

    first = (
        ("x", 2, lambda i: [box(b0 + (low * NY + y) * r0, r0, (high * NX + i) * LANES, LANES)]),
        ("y", 2, lambda i: [box(b0 + (low * NY + i) * r0, r0, high * NX * LANES, NX * LANES)]),
        ("z", 4, lambda i: [box(b0 + (i % NL) * NY * r0, NY * r0, (i // NL) * NX * LANES, NX * LANES)]),
    )
    second = (
        ("y", 2, lambda i: [box(b1 + (low * NY + i) * r1, r1, column(z, x), LANES)]),
        ("z", 2, lambda i: [box(b1 + (i % NL) * NY * r1, NY * r1, column(i, x), LANES)]),
        ("x", 2, lambda i: [box(b1, 16 * r1, (h * NX + i) * LANES, LANES) for h in range(2)]),
    )
    third = (
        ("z", 2, lambda i: [box(b2 + (y * NL + i % NL) * r2, r2, column(i, x), LANES)]),
        ("x", 1, lambda i: [box(b2 + y * NL * r2, NL * r2, (h * NX + i) * LANES, LANES) for h in range(2)]),
        ("y", 4, lambda i: [box(b2 + i * NL * r2, NL * r2, 0, 2 * NX * LANES)]),
    )
    own = (
        (0, r0, aligned(b0 + (low * NY + y) * r0, 16)),
        (r0, r1, aligned(b1 + (low * NY + y) * r1, 16)),
        (r0 + r1, r2, aligned(b2 + (y * NL + low) * r2, 16)),
    )
    return (first, second, third), own, aligned(column(z, x), LANES)


def pieces(boxes, cuts):
    out = []
    for row, count, col, width in boxes:
        start = 0
        for left in range(cuts, 0, -1):
            size = ((count - start) // 16 + left - 1) // left * 16
            out.append((aligned(row + start, 16), size, col, width))
            start += size
    return out


def ring_sends(plans, position, size):
    sends, free = [], {}
    hop, rate = 1.7, 45.0e3
    for colour, stages in enumerate(plans):
        before = []
        for axis, cuts, boxes in stages:
            n, me = size[axis], position[axis]
            now, chain = [], {}
            for s in range(1, n // 2 + 1):
                for way in (1, -1):
                    out = pieces(boxes((me - way * (s - 1) + n) % n), cuts)
                    got = pieces(boxes((me - way * s + n) % n), cuts)
                    middle = len(out) // 2
                    keep = range(len(out))
                    if s == n // 2:
                        keep = keep[:middle] if way == 1 else keep[middle:]
                    for p in keep:
                        needs = before if s == 1 else [chain[way, s - 1, p]]
                        chain[way, s, p] = len(sends)
                        now.append(len(sends))
                        sends.append((colour, axis, way, out[p], got[p], needs))
            before = now
    order, left, arrive = [], set(range(len(sends))), {}
    while left:
        best = None
        for i in left:
            needs = sends[i][5]
            if all(n in arrive for n in needs):
                start = max([arrive[n] for n in needs] + [0.0])
                key = (max(start, free.get(sends[i][1:3], 0.0)), start, i)
                if best is None or key < best:
                    best = key
        at, start, i = best
        left.remove(i)
        _, count, _, width = sends[i][3]
        free[sends[i][1:3]] = at + count * width * 2 / rate
        arrive[i] = at + count * width * 2 / rate + hop
        order.append((start, i))
    order.sort()
    return sends, [i for _, i in order]


def main_kernel(
    rows, chunk, inverse, scale_up,
    block_ref, cent_ref, weighted_ref, counts_ref,
    embed, cents, expo, prob, maxima, logs, total, heard, other_sum, own_sum, other_count, sent_count,
    send_sem, recv_sem, local_sem, cent_sem, lse_send, lse_recv, out_sem,
):
    x, y, z, core = coordinates()
    here = {"x": x, "y": y, "z": z}
    size = {"x": NX, "y": NY, "z": NZ}

    def at(axis, value):
        place = dict(here)
        place[axis] = value
        return device(place["x"], place["y"], place["z"], core)

    mate = device(x, y, z, 1 - core)
    peers = [mate]
    for axis in "xyz":
        peers += [at(axis, (here[axis] + i) % size[axis]) for i in range(1, size[axis])]
    greet(peers)

    colours, own, own_col = gather_plan(rows, x, y, z)
    local = []
    for i, (start, count, row) in enumerate(own):
        local.append(pltpu.make_async_copy(
            block_ref.at[pl.ds(start, count), :],
            embed.at[pl.ds(row, count), pl.ds(own_col, LANES)],
            local_sem.at[i],
        ))
    per = cent_ref.shape[0]
    mine, theirs = aligned(core * per, 256), aligned((1 - core) * per, 256)
    for c in range(8):
        local.append(pltpu.make_async_copy(
            cent_ref.at[:, pl.ds(c * LANES, LANES)],
            cents.at[pl.ds(mine, per), pl.ds(((c % 2) * NX + c // 2) * LANES, LANES)],
            local_sem.at[3 + c],
        ))
    for copy in local:
        copy.start()
    for copy in local:
        copy.wait()

    def view(box):
        row, count, col, width = box
        return embed.at[pl.ds(row, count), pl.ds(col, width)]

    share = pltpu.make_async_remote_copy(
        src_ref=cents.at[pl.ds(mine, per), :], dst_ref=cents.at[pl.ds(mine, per), :],
        send_sem=cent_sem.at[0], recv_sem=cent_sem.at[1], device_id=mate, device_id_type=MESH)
    share.start()
    sends, order = ring_sends(colours, here, size)
    arrived, sent = set(), []

    def remote(i, piece):
        _, axis, way = sends[i][:3]
        return pltpu.make_async_remote_copy(
            src_ref=view(piece), dst_ref=view(piece), send_sem=send_sem.at[i], recv_sem=recv_sem.at[i],
            device_id=at(axis, (here[axis] + way + size[axis]) % size[axis]), device_id_type=MESH)

    def hear(i):
        if i not in arrived:
            arrived.add(i)
            remote(i, sends[i][4]).wait_recv()

    for i in order:
        for need in sends[i][5]:
            hear(need)
        copy = remote(i, sends[i][3])
        copy.start()
        sent.append(copy)
    for i in order:
        hear(i)
    for copy in sent:
        copy.wait_send()
    share.wait_send()
    pltpu.make_async_remote_copy(
        src_ref=cents.at[pl.ds(theirs, per), :], dst_ref=cents.at[pl.ds(theirs, per), :],
        send_sem=cent_sem.at[0], recv_sem=cent_sem.at[1], device_id=mate, device_id_type=MESH).wait_recv()

    count = embed.shape[0]

    def score(i, _):
        span = pl.ds(aligned(i * chunk, chunk), chunk)
        scores = lax.dot_general(
            cents[...], embed[span, :], (((1,), (1,)), ((), ())), preferred_element_type=jnp.float32
        ) * inverse
        top = jnp.max(scores, axis=0, keepdims=True)
        powers = jnp.exp(scores - top)
        expo[:, span] = powers
        maxima[:, span] = top
        logs[:, span] = top + jnp.log(jnp.sum(powers, axis=0, keepdims=True))
        return 0

    lax.fori_loop(0, count // chunk, score, 0)

    base = 0
    for stage, axis in enumerate("xyz"):
        n, me = size[axis], here[axis]
        source = logs if stage == 0 else total.at[stage - 1]
        copies = []
        for i in range(1, n):
            copies.append(pltpu.make_async_remote_copy(
                src_ref=source, dst_ref=heard.at[base + i - 1], send_sem=lse_send.at[base + i - 1],
                recv_sem=lse_recv.at[base + i - 1], device_id=at(axis, (me + i) % n), device_id_type=MESH))
        for copy in copies:
            copy.start()
        for copy in copies:
            copy.wait_recv()
        parts = [source[...]] + [heard[base + i] for i in range(n - 1)]
        top = functools.reduce(jnp.maximum, parts)
        total[stage] = top + jnp.log(sum(jnp.exp(p - top) for p in parts))
        for copy in copies:
            copy.wait_send()
        base += n - 1
    maxima[...] = jnp.exp(maxima[...] - total[2])

    width = cents.shape[0]
    lanes = 256

    def weigh(i, tally):
        span = pl.ds(aligned(i * chunk, chunk), chunk)
        p = expo[:, span] * maxima[:, span]
        prob[:, span] = p.astype(jnp.bfloat16)
        return tally + sum(p[:, j * LANES:(j + 1) * LANES] for j in range(chunk // LANES))

    tally = lax.fori_loop(0, count // chunk, weigh, jnp.zeros((width, LANES), jnp.float32))
    tally = scale_up * jnp.sum(tally.T, axis=0, keepdims=True)
    sent_count[...] = tally

    def product(start, j):
        return scale_up * lax.dot_general(
            prob[pl.ds(start, per), :], embed[:, j * lanes:(j + 1) * lanes],
            (((1,), (0,)), ((), ())), preferred_element_type=jnp.float32)

    give = []
    for j in range(embed.shape[1] // lanes):
        cols = pl.ds(j * lanes, lanes)
        own_sum[:, cols] = product(theirs, j)
        give.append(pltpu.make_async_remote_copy(
            src_ref=own_sum.at[:, cols], dst_ref=other_sum.at[:, cols], send_sem=out_sem.at[0, j],
            recv_sem=out_sem.at[1, j], device_id=mate, device_id_type=MESH))
        give[-1].start()
    give.append(pltpu.make_async_remote_copy(
        src_ref=sent_count, dst_ref=other_count, send_sem=out_sem.at[0, 4],
        recv_sem=out_sem.at[1, 4], device_id=mate, device_id_type=MESH))
    give[-1].start()
    for j in range(embed.shape[1] // lanes):
        part = product(mine, j)
        give[j].wait_recv()
        part = part + other_sum[:, j * lanes:(j + 1) * lanes]
        for b in range(lanes // LANES):
            q = j * (lanes // LANES) + b
            c = (q % NX) * 2 + q // NX
            weighted_ref[:, c * LANES:(c + 1) * LANES] = part[:, b * LANES:(b + 1) * LANES]
    give[-1].wait_recv()
    counts_ref[...] = sent_count[:, pl.ds(mine, per)] + other_count[:, pl.ds(mine, per)]
    for copy in give:
        copy.wait_send()


def cluster(block, centroids, passages):
    per, embed_width = centroids.shape
    centres = per * lax.axis_size("dp") * lax.axis_size("cent")
    part = block.shape[0]
    r0 = part // 3 // 16 * 16
    r1 = (part - r0) // 32 * 16
    rows = (r0, r1, part - r0 - r1)
    count = passages // 2
    vmem = pl.BlockSpec(memory_space=pltpu.VMEM)
    hbm = pl.BlockSpec(memory_space=pl.ANY)
    slots = 128
    weighted, counts = pl.pallas_call(
        functools.partial(main_kernel, rows, 256, 1.0 / (math.sqrt(embed_width) * 0.05), centres / passages),
        out_shape=(
            jax.ShapeDtypeStruct((per, embed_width), jnp.float32),
            jax.ShapeDtypeStruct((1, per), jnp.float32),
        ),
        in_specs=[hbm, hbm],
        out_specs=(vmem, vmem),
        scratch_shapes=[
            pltpu.VMEM((count, embed_width), jnp.bfloat16),
            pltpu.VMEM((2 * per, embed_width), jnp.bfloat16),
            pltpu.VMEM((2 * per, count), jnp.float32),
            pltpu.VMEM((2 * per, count), jnp.bfloat16),
            pltpu.VMEM((1, count), jnp.float32),
            pltpu.VMEM((1, count), jnp.float32),
            pltpu.VMEM((3, 1, count), jnp.float32),
            pltpu.VMEM((NX + NY + NZ - 3, 1, count), jnp.float32),
            pltpu.VMEM((per, embed_width), jnp.float32),
            pltpu.VMEM((per, embed_width), jnp.float32),
            pltpu.VMEM((1, 2 * per), jnp.float32),
            pltpu.VMEM((1, 2 * per), jnp.float32),
            pltpu.SemaphoreType.DMA((slots,)),
            pltpu.SemaphoreType.DMA((slots,)),
            pltpu.SemaphoreType.DMA((11,)),
            pltpu.SemaphoreType.DMA((2,)),
            pltpu.SemaphoreType.DMA((NX + NY + NZ - 3,)),
            pltpu.SemaphoreType.DMA((NX + NY + NZ - 3,)),
            pltpu.SemaphoreType.DMA((2, 5)),
        ],
        compiler_params=pltpu.CompilerParams(
            collective_id=0, has_side_effects=True, vmem_limit_bytes=60 * 1024 * 1024),
        name="cluster",
    )(block, centroids)
    return weighted, counts.reshape(per)


def encode_kernel(
    hidden_ref, residual_ref, down_ref, gain_ref, proj_ref, block_ref,
    down, hid, res, scale, proj, part, relayed, heard, given, heard_f, normed, turned,
    sums_x, relayed_x, heard_x, sums_h, heard_h, square, squares,
    send_sem, recv_sem, local_sem, part_send, part_recv,
):
    x, y, z, core = coordinates()
    low, high = z % NL, z // NL
    mate = device(x, y, z, 1 - core)
    far = device(x, y, (z + NL) % NZ, core)
    turn = device(y, x, z, core)
    alone = x == y

    def at_x(i):
        return device((x + i) % NX, y, z, core)

    def at_far(i):
        return device((x + i) % NX, y, (z + NL) % NZ, core)

    def at_y(i):
        return device(x, (y + i) % NY, z, core)

    def at_low(i):
        return device(x, y, high * NL + (low + i) % NL, core)

    peers = [mate, far] + [f(i) for f in (at_x, at_far, at_y, at_low) for i in (1, 2, 3)]
    barrier = pltpu.get_barrier_semaphore()
    for peer in peers:
        pl.semaphore_signal(barrier, inc=1, device_id=peer, device_id_type=MESH)

    @pl.when(jnp.logical_not(alone))
    def _():
        pl.semaphore_signal(barrier, inc=1, device_id=turn, device_id_type=MESH)

    pl.semaphore_wait(barrier, jnp.where(alone, len(peers), len(peers) + 1))

    used, done, kept = [0], [], []

    def remote(src, dst, target, start=True):
        i = used[0]
        used[0] += 1
        copy = pltpu.make_async_remote_copy(
            src_ref=src, dst_ref=dst, send_sem=send_sem.at[i], recv_sem=recv_sem.at[i],
            device_id=target, device_id_type=MESH)
        if start:
            copy.start()
            done.append(copy)
        return copy

    def local(src, dst, start=True):
        copy = pltpu.make_async_copy(src, dst, local_sem.at[len(kept)])
        kept.append(copy)
        if start:
            copy.start()
        return copy

    def transposed(src, dst):
        out, here = remote(src, dst, turn, False), local(src, dst, False)

        @pl.when(jnp.logical_not(alone))
        def _():
            out.start()

        @pl.when(alone)
        def _():
            here.start()

        return out, here

    def land(pair):
        @pl.when(jnp.logical_not(alone))
        def _():
            pair[0].wait()

        @pl.when(alone)
        def _():
            pair[1].wait()

    mine = pl.ds(aligned(core * LANES, LANES), LANES)
    passages = hidden_ref.shape[0]
    wide = 2 * LANES

    own = down.at[low, :, mine]
    along_z = {i: remote(down_ref, own, at_low(i)) for i in (1, 3, 2)}
    along_y = [remote(hidden_ref, hid.at[y], at_y(i)) for i in (1, 3)]
    crossed = {0: remote(down_ref, own, mate)}
    first = [local(down_ref, own), local(hidden_ref, hid.at[y])]
    loaded = local(proj_ref, proj)
    moved = [transposed(residual_ref, res), transposed(gain_ref, scale)]

    for copy in along_y:
        copy.wait_recv()
    upper = (passages // 2 + 15) // 16 * 16
    lower = hid.at[(y + 3) % NY, pl.ds(0, upper), :]
    along_y = [remote(lower, lower, at_y(1))]
    lower = hid.at[(y + 1) % NY, pl.ds(upper, passages - upper), :]
    along_y.append(remote(lower, lower, at_y(3)))
    for copy in first:
        copy.wait()
    for copy in along_y:
        copy.wait_recv()
    flat = (NY * passages, hid.shape[2])
    sent = []
    cut = passages // 2
    spans = (pl.ds(0, cut), pl.ds(cut, passages - cut))

    def scatter(view, relay, got, send, recv):
        def copies(i):
            way = 1 if i % 2 == 0 else 3
            if i < 2:
                src, dst = view((x + 2) % NX).at[spans[i], :], relay(i)
            else:
                src, dst = view((x + way) % NX), got(i - 2)
            return pltpu.make_async_remote_copy(
                src_ref=src, dst_ref=dst, send_sem=send(i), recv_sem=recv(i),
                device_id=at_x(way), device_id_type=MESH)

        def start(i):
            copy = copies(i)
            copy.start()
            sent.append(copy)

        def first():
            start(0)
            start(1)

        def second():
            for i, way in ((0, 1), (1, 3)):
                copies(i).wait_recv()
                target = view((x + way) % NX)
                target[spans[i], :] = target[spans[i], :] + relay(i)[...]
                start(2 + i)

        def finish():
            copies(2).wait_recv()
            copies(3).wait_recv()
            return view(x)[...] + got(0)[...] + got(1)[...]

        return first, second, finish

    def block_scatter(zc):
        return scatter(
            lambda q: part.at[zc, q], lambda i: relayed.at[zc, i], lambda i: heard.at[zc, i],
            lambda i: part_send.at[zc, i], lambda i: part_recv.at[zc, i])

    waiting = None
    for zi in (0, 1, 3, 2):
        zc = (low - zi + NL) % NL
        if zi:
            along_z[zi].wait_recv()
            crossed[zi] = remote(down.at[zc, :, mine], down.at[zc, :, mine], mate)
        crossed[zi].wait_recv()
        value = jnp.dot(hid[...].reshape(flat), down[zc], preferred_element_type=jnp.float32)
        for q in range(NX):
            part[zc, q] = value[q * passages:(q + 1) * passages]
        first, second, _ = block_scatter(zc)
        first()
        if waiting is not None:
            waiting()
        waiting = second
    waiting()

    def over_x(zc):
        return block_scatter(zc)[2]()

    others = []
    for b in range(2):
        given[b] = over_x((1 - high) * 2 + b)
        others.append(remote(given.at[b], heard_f.at[b], far))
    for pair in moved:
        land(pair)
    for b in range(2):
        value = over_x(high * 2 + b)
        others[b].wait_recv()
        cols = pl.ds(b * wide, wide)
        gain = jnp.concatenate([scale[2 * b], scale[2 * b + 1]], axis=1)
        value = value + heard_f[b] + res[:, cols].astype(jnp.float32)
        normed[:, cols] = (value * gain).astype(jnp.bfloat16)
    land(transposed(normed, turned))
    loaded.wait()
    mixed = jnp.dot(turned[...], proj[...], preferred_element_type=jnp.float32)
    for q in range(NX):
        sums_x[q] = mixed[:, q * wide:(q + 1) * wide]
    first, second, finish = scatter(
        lambda q: sums_x.at[q], lambda i: relayed_x.at[i], lambda i: heard_x.at[i],
        lambda i: part_send.at[NL, i], lambda i: part_recv.at[NL, i])
    first()
    second()
    value = finish()
    for h in range(2):
        sums_h[h] = value[:, h * LANES:(h + 1) * LANES]
    remote(sums_h.at[1 - high], heard_h, far).wait_recv()
    value = sums_h[high] + heard_h[...]

    pad = square.shape[1] - passages
    squared = jnp.concatenate([value * value, jnp.zeros((pad, LANES), jnp.float32)], axis=0)
    square[...] = jnp.sum(squared.T, axis=0, keepdims=True)
    stage = [remote(square, squares.at[i - 1], at_x(i)) for i in (1, 2, 3)]
    stage += [remote(square, squares.at[3 + i], at_far(i)) for i in range(4)]
    for copy in stage:
        copy.wait_recv()
    total = square[...]
    for i in range(7):
        total = total + squares[i]
    norm = lax.rsqrt(total * (1.0 / proj_ref.shape[1]) + 1e-06)
    norm = jnp.broadcast_to(norm, (LANES, norm.shape[1])).T
    block_ref[...] = (value * norm[:passages]).astype(jnp.bfloat16)

    for copy in sent + done:
        copy.wait_send()


def encode(hidden, residual, down_weight, gain, proj_weight):
    passages, units = hidden.shape
    features, embed_width = proj_weight.shape
    vmem = pl.BlockSpec(memory_space=pltpu.VMEM)
    hbm = pl.BlockSpec(memory_space=pl.ANY)
    bf16, f32 = jnp.bfloat16, jnp.float32
    wide = 2 * LANES
    padded = (passages + LANES - 1) // LANES * LANES
    slots = 3 + 4 + 4 + 3 + 2 + 1 + 7
    return pl.pallas_call(
        encode_kernel,
        out_shape=jax.ShapeDtypeStruct((passages, LANES), bf16),
        in_specs=[hbm, hbm, hbm, hbm, hbm],
        out_specs=vmem,
        scratch_shapes=[
            pltpu.VMEM((NL, units, wide), bf16),
            pltpu.VMEM((NY, passages, units), bf16),
            pltpu.VMEM((passages, features), bf16),
            pltpu.VMEM((features // LANES, 1, LANES), f32),
            pltpu.VMEM((features, embed_width), bf16),
            pltpu.VMEM((NL, NX, passages, wide), f32),
            pltpu.VMEM((NL, 2, passages // 2, wide), f32),
            pltpu.VMEM((NL, 2, passages, wide), f32),
            pltpu.VMEM((2, passages, wide), f32),
            pltpu.VMEM((2, passages, wide), f32),
            pltpu.VMEM((passages, features), bf16),
            pltpu.VMEM((passages, features), bf16),
            pltpu.VMEM((NX, passages, wide), f32),
            pltpu.VMEM((2, passages // 2, wide), f32),
            pltpu.VMEM((2, passages, wide), f32),
            pltpu.VMEM((2, passages, LANES), f32),
            pltpu.VMEM((passages, LANES), f32),
            pltpu.VMEM((1, padded), f32),
            pltpu.VMEM((7, 1, padded), f32),
            pltpu.SemaphoreType.DMA((slots,)),
            pltpu.SemaphoreType.DMA((slots,)),
            pltpu.SemaphoreType.DMA((6,)),
            pltpu.SemaphoreType.DMA((NL + 1, 4)),
            pltpu.SemaphoreType.DMA((NL + 1, 4)),
        ],
        compiler_params=pltpu.CompilerParams(
            collective_id=1, has_side_effects=True, vmem_limit_bytes=63 * 1024 * 1024),
        name="encode",
    )(hidden, residual, down_weight, gain.reshape(features // LANES, 1, LANES), proj_weight)


def body(hidden, residual, down_weight, gain, proj_weight, centroids):
    block = encode(hidden, residual, down_weight, gain, proj_weight)
    return cluster(block, centroids, hidden.shape[0] * lax.axis_size("dp"))


def solution(mesh):
    in_specs = (
        P("dp", "cent"),
        P("dp", "cent"),
        P("cent", "dp"),
        P("cent"),
        P("cent", None),
        P(("dp", "cent"), None),
    )
    out_specs = (P(("dp", "cent"), None), P(("dp", "cent")))
    return jax.shard_map(body, mesh=mesh, in_specs=in_specs, out_specs=out_specs, check_vma=False)
```

```python
import functools
import math

import jax
import jax.numpy as jnp
from jax import lax
from jax.experimental import pallas as pl
from jax.experimental.pallas import tpu as pltpu
from jax.sharding import PartitionSpec as P

MESH = pl.DeviceIdType.MESH
NX, NY, NZ = 4, 4, 8
NL = 4
LANES = 128


def coordinates():
    dp, cent = lax.axis_index("dp"), lax.axis_index("cent")
    y, low, core = dp // (2 * NL), (dp // 2) % NL, dp % 2
    return cent // 2, y, (cent % 2) * NL + low, core


def device(x, y, z, core):
    return (y * (2 * NL) + (z % NL) * 2 + core, x * 2 + z // NL)


def aligned(value, multiple):
    return pl.multiple_of(value, multiple)


def gather_plan(rows, x, y, z):
    low, high = z % NL, z // NL
    r0, r1, r2 = rows
    b0, b1, b2 = 0, 16 * r0, 16 * (r0 + r1)

    def box(row, count, col, width):
        return (aligned(row, 16), count, aligned(col, LANES), width)

    def column(zc, xc):
        return ((zc // NL) * NX + xc) * LANES

    first = (
        ("x", 2, lambda i: [box(b0 + (low * NY + y) * r0, r0, (high * NX + i) * LANES, LANES)]),
        ("y", 2, lambda i: [box(b0 + (low * NY + i) * r0, r0, high * NX * LANES, NX * LANES)]),
        ("z", 4, lambda i: [box(b0 + (i % NL) * NY * r0, NY * r0, (i // NL) * NX * LANES, NX * LANES)]),
    )
    second = (
        ("y", 2, lambda i: [box(b1 + (low * NY + i) * r1, r1, column(z, x), LANES)]),
        ("z", 2, lambda i: [box(b1 + (i % NL) * NY * r1, NY * r1, column(i, x), LANES)]),
        ("x", 2, lambda i: [box(b1, 16 * r1, (h * NX + i) * LANES, LANES) for h in range(2)]),
    )
    third = (
        ("z", 2, lambda i: [box(b2 + (y * NL + i % NL) * r2, r2, column(i, x), LANES)]),
        ("x", 1, lambda i: [box(b2 + y * NL * r2, NL * r2, (h * NX + i) * LANES, LANES) for h in range(2)]),
        ("y", 4, lambda i: [box(b2 + i * NL * r2, NL * r2, 0, 2 * NX * LANES)]),
    )
    own = (
        (0, r0, aligned(b0 + (low * NY + y) * r0, 16)),
        (r0, r1, aligned(b1 + (low * NY + y) * r1, 16)),
        (r0 + r1, r2, aligned(b2 + (y * NL + low) * r2, 16)),
    )
    return (first, second, third), own, aligned(column(z, x), LANES)


def pieces(boxes, cuts):
    out = []
    for row, count, col, width in boxes:
        start = 0
        for left in range(cuts, 0, -1):
            size = ((count - start) // 16 + left - 1) // left * 16
            out.append((aligned(row + start, 16), size, col, width))
            start += size
    return out


def ring_sends(plans, position, size):
    sends, free = [], {}
    hop, rate = 1.7, 45.0e3
    for colour, stages in enumerate(plans):
        before = []
        for axis, cuts, boxes in stages:
            n, me = size[axis], position[axis]
            now, chain = [], {}
            for s in range(1, n // 2 + 1):
                for way in (1, -1):
                    out = pieces(boxes((me - way * (s - 1) + n) % n), cuts)
                    got = pieces(boxes((me - way * s + n) % n), cuts)
                    middle = len(out) // 2
                    keep = range(len(out))
                    if s == n // 2:
                        keep = keep[:middle] if way == 1 else keep[middle:]
                    for p in keep:
                        needs = before if s == 1 else [chain[way, s - 1, p]]
                        chain[way, s, p] = len(sends)
                        now.append(len(sends))
                        sends.append((colour, axis, way, out[p], got[p], needs))
            before = now
    order, left, arrive = [], set(range(len(sends))), {}
    while left:
        best = None
        for i in left:
            needs = sends[i][5]
            if all(n in arrive for n in needs):
                start = max([arrive[n] for n in needs] + [0.0])
                key = (max(start, free.get(sends[i][1:3], 0.0)), start, i)
                if best is None or key < best:
                    best = key
        at, start, i = best
        left.remove(i)
        _, count, _, width = sends[i][3]
        free[sends[i][1:3]] = at + count * width * 2 / rate
        arrive[i] = at + count * width * 2 / rate + hop
        order.append((start, i))
    order.sort()
    return sends, [i for _, i in order]


def cluster(
    rows, chunk, inverse, scale_up, value, weighted_ref, counts_ref,
    embed, cents, expo, prob, maxima, logs, total, heard, other_sum, own_sum, kept_sum, tally, other_count, sent_count,
    send_sem, recv_sem, lse_send, lse_recv, out_sem,
):
    x, y, z, core = coordinates()
    here = {"x": x, "y": y, "z": z}
    size = {"x": NX, "y": NY, "z": NZ}
    mate = device(x, y, z, 1 - core)
    per = weighted_ref.shape[0]
    mine, theirs = aligned(core * per, 256), aligned((1 - core) * per, 256)

    def at(axis, value):
        place = dict(here)
        place[axis] = value
        return device(place["x"], place["y"], place["z"], core)

    colours, own, own_col = gather_plan(rows, x, y, z)
    for start, count, row in own:
        embed[pl.ds(row, count), pl.ds(own_col, LANES)] = value[start:start + count]

    def view(box):
        row, count, col, width = box
        return embed.at[pl.ds(row, count), pl.ds(col, width)]

    sends, order = ring_sends(colours, here, size)
    arrived, sent = set(), []

    def remote(i, piece):
        _, axis, way = sends[i][:3]
        return pltpu.make_async_remote_copy(
            src_ref=view(piece), dst_ref=view(piece), send_sem=send_sem.at[i], recv_sem=recv_sem.at[i],
            device_id=at(axis, (here[axis] + way + size[axis]) % size[axis]), device_id_type=MESH)

    def hear(i):
        if i not in arrived:
            arrived.add(i)
            remote(i, sends[i][4]).wait_recv()

    for i in order:
        for need in sends[i][5]:
            hear(need)
        copy = remote(i, sends[i][3])
        copy.start()
        sent.append(copy)

    groups, start = [], 0
    for r in rows:
        groups.append((start, NY * NL * r))
        start += NY * NL * r

    def score(g):
        start, count = groups[g]
        span = pl.ds(start, count)
        scores = lax.dot_general(
            cents[...], embed[span, :], (((1,), (1,)), ((), ())), preferred_element_type=jnp.float32
        ) * inverse
        top = jnp.max(scores, axis=0, keepdims=True)
        powers = jnp.exp(scores - top)
        expo[:, span] = powers
        maxima[:, span] = top
        logs[:, span] = top + jnp.log(jnp.sum(powers, axis=0, keepdims=True))

    bases = {"x": 0, "y": NX - 1, "z": NX + NY - 2}

    def exchange(g, stage):
        axis, span = "xyz"[stage], pl.ds(*groups[g])
        source = (logs if stage == 0 else total.at[stage - 1]).at[:, span]
        copies = []
        for i in range(1, size[axis]):
            slot = bases[axis] + i - 1
            copies.append(pltpu.make_async_remote_copy(
                src_ref=source, dst_ref=heard.at[slot, :, span], send_sem=lse_send.at[g, slot],
                recv_sem=lse_recv.at[g, slot], device_id=at(axis, (here[axis] + i) % size[axis]),
                device_id_type=MESH))
        return source, copies

    def tell(g, stage):
        for copy in exchange(g, stage)[1]:
            copy.start()
            sent.append(copy)

    def learn(g, stage):
        source, copies = exchange(g, stage)
        span = pl.ds(*groups[g])
        for copy in copies:
            copy.wait_recv()
        base = bases["xyz"[stage]]
        parts = [source[...]] + [heard[base + i, :, span] for i in range(len(copies))]
        top = functools.reduce(jnp.maximum, parts)
        total[stage, :, span] = top + jnp.log(sum(jnp.exp(p - top) for p in parts))

    def weigh(g):
        start, count = groups[g]
        whole = pl.ds(start, count)
        maxima[:, whole] = jnp.exp(maxima[:, whole] - total[2, :, whole])

        def step(i, running):
            span = pl.ds(aligned(start + i * chunk, chunk), chunk)
            p = expo[:, span] * maxima[:, span]
            prob[:, span] = p.astype(jnp.bfloat16)
            return running + sum(p[:, j * LANES:(j + 1) * LANES] for j in range(chunk // LANES))

        first = jnp.zeros(tally.shape, jnp.float32) if g == 0 else tally[...]
        tally[...] = lax.fori_loop(0, count // chunk, step, first)

    lanes = 256

    def product(g, first, j):
        start, count = groups[g]
        return lax.dot_general(
            prob[pl.ds(first, per), pl.ds(start, count)], embed[pl.ds(start, count), j * lanes:(j + 1) * lanes],
            (((1,), (0,)), ((), ())), preferred_element_type=jnp.float32)

    blocks = embed.shape[1] // lanes

    def accumulate(g):
        for j in range(blocks):
            cols = pl.ds(j * lanes, lanes)
            for first, ref in ((theirs, own_sum), (mine, kept_sum)):
                value = product(g, first, j)
                ref[:, cols] = value if g == 0 else ref[:, cols] + value

    def ends(c):
        for i in order:
            if sends[i][0] == c:
                hear(i)

    ends(0)
    score(0)
    tell(0, 0)
    ends(1)
    score(1)
    tell(1, 0)
    learn(0, 0)
    tell(0, 1)
    ends(2)
    score(2)
    tell(2, 0)
    learn(1, 0)
    tell(1, 1)
    learn(0, 1)
    tell(0, 2)
    learn(2, 0)
    tell(2, 1)
    learn(1, 1)
    tell(1, 2)
    learn(0, 2)
    weigh(0)
    learn(2, 1)
    tell(2, 2)
    accumulate(0)
    learn(1, 2)
    weigh(1)
    accumulate(1)
    learn(2, 2)
    weigh(2)
    sent_count[...] = scale_up * jnp.sum(tally[...].T, axis=0, keepdims=True)

    give = [pltpu.make_async_remote_copy(
        src_ref=sent_count, dst_ref=other_count, send_sem=out_sem.at[0, blocks],
        recv_sem=out_sem.at[1, blocks], device_id=mate, device_id_type=MESH)]
    give[0].start()
    for j in range(blocks):
        cols = pl.ds(j * lanes, lanes)
        own_sum[:, cols] = scale_up * (own_sum[:, cols] + product(2, theirs, j))
        give.append(pltpu.make_async_remote_copy(
            src_ref=own_sum.at[:, cols], dst_ref=other_sum.at[:, cols], send_sem=out_sem.at[0, j],
            recv_sem=out_sem.at[1, j], device_id=mate, device_id_type=MESH))
        give[-1].start()
    for j in range(blocks):
        cols = pl.ds(j * lanes, lanes)
        part = scale_up * (kept_sum[:, cols] + product(2, mine, j))
        give[1 + j].wait_recv()
        part = part + other_sum[:, cols]
        for b in range(lanes // LANES):
            q = j * (lanes // LANES) + b
            c = (q % NX) * 2 + q // NX
            weighted_ref[:, c * LANES:(c + 1) * LANES] = part[:, b * LANES:(b + 1) * LANES]
    give[0].wait_recv()
    counts_ref[...] = sent_count[:, pl.ds(mine, per)] + other_count[:, pl.ds(mine, per)]
    for copy in give + sent:
        copy.wait_send()


def encode(
    early, later, hidden_ref, residual_ref, down_ref, gain_ref, proj_ref,
    down, hid, res, scale, proj, part, relayed, heard, given, heard_f, normed, turned,
    sums_x, relayed_x, heard_x, sums_h, heard_h, square, squares,
    send_sem, recv_sem, local_sem, part_send, part_recv,
):
    x, y, z, core = coordinates()
    low, high = z % NL, z // NL
    mate = device(x, y, z, 1 - core)
    far = device(x, y, (z + NL) % NZ, core)
    turn = device(y, x, z, core)
    alone = x == y

    def at_x(i):
        return device((x + i) % NX, y, z, core)

    def at_far(i):
        return device((x + i) % NX, y, (z + NL) % NZ, core)

    def at_y(i):
        return device(x, (y + i) % NY, z, core)

    def at_low(i):
        return device(x, y, high * NL + (low + i) % NL, core)

    peers = [mate] + [f(i) for f in (at_x, at_far, at_y) for i in (1, 2, 3)]
    peers += [device(x, y, (z + i) % NZ, core) for i in range(1, NZ)]
    barrier = pltpu.get_barrier_semaphore()
    for peer in peers:
        pl.semaphore_signal(barrier, inc=1, device_id=peer, device_id_type=MESH)

    @pl.when(jnp.logical_not(alone))
    def _():
        pl.semaphore_signal(barrier, inc=1, device_id=turn, device_id_type=MESH)

    pl.semaphore_wait(barrier, jnp.where(alone, len(peers), len(peers) + 1))

    used, done, kept = [0], [], []

    def remote(src, dst, target, start=True):
        i = used[0]
        used[0] += 1
        copy = pltpu.make_async_remote_copy(
            src_ref=src, dst_ref=dst, send_sem=send_sem.at[i], recv_sem=recv_sem.at[i],
            device_id=target, device_id_type=MESH)
        if start:
            copy.start()
            done.append(copy)
        return copy

    def local(src, dst, start=True):
        copy = pltpu.make_async_copy(src, dst, local_sem.at[len(kept)])
        kept.append(copy)
        if start:
            copy.start()
        return copy

    def transposed(src, dst):
        out, here = remote(src, dst, turn, False), local(src, dst, False)

        @pl.when(jnp.logical_not(alone))
        def _():
            out.start()

        @pl.when(alone)
        def _():
            here.start()

        return out, here

    def land(pair):
        @pl.when(jnp.logical_not(alone))
        def _():
            pair[0].wait()

        @pl.when(alone)
        def _():
            pair[1].wait()

    mine = pl.ds(aligned(core * LANES, LANES), LANES)
    passages = hidden_ref.shape[0]
    wide = 2 * LANES

    own = down.at[low, :, mine]
    along_z = {i: remote(down_ref, own, at_low(i)) for i in (1, 3, 2)}
    along_y = [remote(hidden_ref, hid.at[y], at_y(i)) for i in (1, 3)]
    crossed = {0: remote(down_ref, own, mate)}
    first = [local(down_ref, own), local(hidden_ref, hid.at[y])]
    loaded = local(proj_ref, proj)
    moved = [transposed(residual_ref, res), transposed(gain_ref, scale)]
    early()

    for copy in along_y:
        copy.wait_recv()
    upper = (passages // 2 + 15) // 16 * 16
    lower = hid.at[(y + 3) % NY, pl.ds(0, upper), :]
    along_y = [remote(lower, lower, at_y(1))]
    lower = hid.at[(y + 1) % NY, pl.ds(upper, passages - upper), :]
    along_y.append(remote(lower, lower, at_y(3)))
    for copy in first:
        copy.wait()
    for copy in along_y:
        copy.wait_recv()
    flat = (NY * passages, hid.shape[2])
    sent = []
    cut = passages // 2
    spans = (pl.ds(0, cut), pl.ds(cut, passages - cut))

    def scatter(view, relay, got, send, recv):
        def copies(i):
            way = 1 if i % 2 == 0 else 3
            if i < 2:
                src, dst = view((x + 2) % NX).at[spans[i], :], relay(i)
            else:
                src, dst = view((x + way) % NX), got(i - 2)
            return pltpu.make_async_remote_copy(
                src_ref=src, dst_ref=dst, send_sem=send(i), recv_sem=recv(i),
                device_id=at_x(way), device_id_type=MESH)

        def start(i):
            copy = copies(i)
            copy.start()
            sent.append(copy)

        def first():
            start(0)
            start(1)

        def second():
            for i, way in ((0, 1), (1, 3)):
                copies(i).wait_recv()
                target = view((x + way) % NX)
                target[spans[i], :] = target[spans[i], :] + relay(i)[...]
                start(2 + i)

        def finish():
            copies(2).wait_recv()
            copies(3).wait_recv()
            return view(x)[...] + got(0)[...] + got(1)[...]

        return first, second, finish

    def block_scatter(zc):
        return scatter(
            lambda q: part.at[zc, q], lambda i: relayed.at[zc, i], lambda i: heard.at[zc, i],
            lambda i: part_send.at[zc, i], lambda i: part_recv.at[zc, i])

    waiting = None
    for zi in (0, 1, 3, 2):
        zc = (low - zi + NL) % NL
        if zi:
            along_z[zi].wait_recv()
            crossed[zi] = remote(down.at[zc, :, mine], down.at[zc, :, mine], mate)
        crossed[zi].wait_recv()
        value = jnp.dot(hid[...].reshape(flat), down[zc], preferred_element_type=jnp.float32)
        for q in range(NX):
            part[zc, q] = value[q * passages:(q + 1) * passages]
        first, second, _ = block_scatter(zc)
        first()
        if waiting is not None:
            waiting()
        waiting = second
    waiting()

    def over_x(zc):
        return block_scatter(zc)[2]()

    later()
    others = []
    for b in range(2):
        given[b] = over_x((1 - high) * 2 + b)
        others.append(remote(given.at[b], heard_f.at[b], far))
    for pair in moved:
        land(pair)
    for b in range(2):
        value = over_x(high * 2 + b)
        others[b].wait_recv()
        cols = pl.ds(b * wide, wide)
        gain = jnp.concatenate([scale[2 * b], scale[2 * b + 1]], axis=1)
        value = value + heard_f[b] + res[:, cols].astype(jnp.float32)
        normed[:, cols] = (value * gain).astype(jnp.bfloat16)
    land(transposed(normed, turned))
    loaded.wait()
    mixed = jnp.dot(turned[...], proj[...], preferred_element_type=jnp.float32)
    for q in range(NX):
        sums_x[q] = mixed[:, q * wide:(q + 1) * wide]
    first, second, finish = scatter(
        lambda q: sums_x.at[q], lambda i: relayed_x.at[i], lambda i: heard_x.at[i],
        lambda i: part_send.at[NL, i], lambda i: part_recv.at[NL, i])
    first()
    second()
    value = finish()
    for h in range(2):
        sums_h[h] = value[:, h * LANES:(h + 1) * LANES]
    remote(sums_h.at[1 - high], heard_h, far).wait_recv()
    value = sums_h[high] + heard_h[...]

    pad = square.shape[1] - passages
    squared = jnp.concatenate([value * value, jnp.zeros((pad, LANES), jnp.float32)], axis=0)
    square[...] = jnp.sum(squared.T, axis=0, keepdims=True)
    stage = [remote(square, squares.at[i - 1], at_x(i)) for i in (1, 2, 3)]
    stage += [remote(square, squares.at[3 + i], at_far(i)) for i in range(4)]
    for copy in stage:
        copy.wait_recv()
    total = square[...]
    for i in range(7):
        total = total + squares[i]
    norm = lax.rsqrt(total * (1.0 / proj_ref.shape[1]) + 1e-06)
    norm = jnp.broadcast_to(norm, (LANES, norm.shape[1])).T
    for copy in sent + done:
        copy.wait_send()
    return (value * norm[:passages]).astype(jnp.bfloat16)


def whole_kernel(
    split, plan, hidden_ref, residual_ref, down_ref, gain_ref, proj_ref, cent_ref, weighted_ref, counts_ref, *scratch,
):
    cent_local, cent_sem, *scratch = scratch
    encoder, rest = scratch[:split], scratch[split:]
    cents = rest[1]
    x, y, z, core = coordinates()
    per = cent_ref.shape[0]
    mine, theirs = (pl.ds(aligned(c * per, 256), per) for c in (core, 1 - core))

    def shared(rows):
        return pltpu.make_async_remote_copy(
            src_ref=cents.at[rows, :], dst_ref=cents.at[rows, :], send_sem=cent_sem.at[0],
            recv_sem=cent_sem.at[1], device_id=device(x, y, z, 1 - core), device_id_type=MESH)

    copies = [
        pltpu.make_async_copy(
            cent_ref.at[:, pl.ds(c * LANES, LANES)],
            cents.at[mine, pl.ds(((c % 2) * NX + c // 2) * LANES, LANES)],
            cent_local.at[c])
        for c in range(2 * NX)
    ]

    def early():
        for copy in copies:
            copy.start()

    def later():
        for copy in copies:
            copy.wait()
        shared(mine).start()

    value = encode(early, later, hidden_ref, residual_ref, down_ref, gain_ref, proj_ref, *encoder)
    shared(theirs).wait_recv()
    shared(mine).wait_send()
    cluster(*plan, value, weighted_ref, counts_ref, *rest)


def body(hidden, residual, down_weight, gain, proj_weight, centroids):
    passages, units = hidden.shape
    features, embed_width = proj_weight.shape
    per = centroids.shape[0]
    everyone = passages * lax.axis_size("dp")
    centres = per * lax.axis_size("dp") * lax.axis_size("cent")
    r0 = passages // 3 // 16 * 16
    r1 = (passages - r0) // 32 * 16
    rows = (r0, r1, passages - r0 - r1)
    count = everyone // 2
    bf16, f32 = jnp.bfloat16, jnp.float32
    vmem = pl.BlockSpec(memory_space=pltpu.VMEM)
    hbm = pl.BlockSpec(memory_space=pl.ANY)
    wide = 2 * LANES
    padded = (passages + LANES - 1) // LANES * LANES
    slots = 3 + 4 + 4 + 3 + 2 + 1 + 7
    hops = NX + NY + NZ - 3
    encoder = [
        pltpu.VMEM((NL, units, wide), bf16),
        pltpu.VMEM((NY, passages, units), bf16),
        pltpu.VMEM((passages, features), bf16),
        pltpu.VMEM((features // LANES, 1, LANES), f32),
        pltpu.VMEM((features, embed_width), bf16),
        pltpu.VMEM((NL, NX, passages, wide), f32),
        pltpu.VMEM((NL, 2, passages // 2, wide), f32),
        pltpu.VMEM((NL, 2, passages, wide), f32),
        pltpu.VMEM((2, passages, wide), f32),
        pltpu.VMEM((2, passages, wide), f32),
        pltpu.VMEM((passages, features), bf16),
        pltpu.VMEM((passages, features), bf16),
        pltpu.VMEM((NX, passages, wide), f32),
        pltpu.VMEM((2, passages // 2, wide), f32),
        pltpu.VMEM((2, passages, wide), f32),
        pltpu.VMEM((2, passages, LANES), f32),
        pltpu.VMEM((passages, LANES), f32),
        pltpu.VMEM((1, padded), f32),
        pltpu.VMEM((7, 1, padded), f32),
        pltpu.SemaphoreType.DMA((slots,)),
        pltpu.SemaphoreType.DMA((slots,)),
        pltpu.SemaphoreType.DMA((6,)),
        pltpu.SemaphoreType.DMA((NL + 1, 4)),
        pltpu.SemaphoreType.DMA((NL + 1, 4)),
    ]
    rest = [
        pltpu.VMEM((count, embed_width), bf16),
        pltpu.VMEM((2 * per, embed_width), bf16),
        pltpu.VMEM((2 * per, count), f32),
        pltpu.VMEM((2 * per, count), bf16),
        pltpu.VMEM((1, count), f32),
        pltpu.VMEM((1, count), f32),
        pltpu.VMEM((3, 1, count), f32),
        pltpu.VMEM((hops, 1, count), f32),
        pltpu.VMEM((per, embed_width), f32),
        pltpu.VMEM((per, embed_width), f32),
        pltpu.VMEM((per, embed_width), f32),
        pltpu.VMEM((2 * per, LANES), f32),
        pltpu.VMEM((1, 2 * per), f32),
        pltpu.VMEM((1, 2 * per), f32),
        pltpu.SemaphoreType.DMA((128,)),
        pltpu.SemaphoreType.DMA((128,)),
        pltpu.SemaphoreType.DMA((3, hops)),
        pltpu.SemaphoreType.DMA((3, hops)),
        pltpu.SemaphoreType.DMA((2, 5)),
    ]
    plan = (rows, 256, 1.0 / (math.sqrt(embed_width) * 0.05), centres / everyone)
    weighted, counts = pl.pallas_call(
        functools.partial(whole_kernel, len(encoder), plan),
        out_shape=(jax.ShapeDtypeStruct((per, embed_width), f32), jax.ShapeDtypeStruct((1, per), f32)),
        in_specs=[hbm] * 6,
        out_specs=(vmem, vmem),
        scratch_shapes=[pltpu.SemaphoreType.DMA((2 * NX,)), pltpu.SemaphoreType.DMA((2,))] + encoder + rest,
        compiler_params=pltpu.CompilerParams(
            collective_id=0, has_side_effects=True, vmem_limit_bytes=63 * 1024 * 1024),
        name="soft_kmeans",
    )(hidden, residual, down_weight, gain.reshape(features // LANES, 1, LANES), proj_weight, centroids)
    return weighted, counts.reshape(per)


def solution(mesh):
    in_specs = (
        P("dp", "cent"),
        P("dp", "cent"),
        P("cent", "dp"),
        P("cent"),
        P("cent", None),
        P(("dp", "cent"), None),
    )
    out_specs = (P(("dp", "cent"), None), P(("dp", "cent")))
    return jax.shard_map(body, mesh=mesh, in_specs=in_specs, out_specs=out_specs, check_vma=False)
```

```python
import functools
import math

import jax
import jax.numpy as jnp
from jax import lax
from jax.experimental import pallas as pl
from jax.experimental.pallas import tpu as pltpu
from jax.sharding import PartitionSpec as P

MESH = pl.DeviceIdType.MESH
NX, NY, NZ = 4, 4, 8
NL = 4
LANES = 128


def coordinates():
    dp, cent = lax.axis_index("dp"), lax.axis_index("cent")
    y, low, core = dp // (2 * NL), (dp // 2) % NL, dp % 2
    return cent // 2, y, (cent % 2) * NL + low, core


def device(x, y, z, core):
    return (y * (2 * NL) + (z % NL) * 2 + core, x * 2 + z // NL)


def aligned(value, multiple):
    return pl.multiple_of(value, multiple)


def gather_plan(rows, x, y, z):
    low, high = z % NL, z // NL
    r0, r1, r2 = rows
    b0, b1, b2 = 0, 16 * r0, 16 * (r0 + r1)

    def box(row, count, col, width):
        return (aligned(row, 16), count, aligned(col, LANES), width)

    def column(zc, xc):
        return ((zc // NL) * NX + xc) * LANES

    first = (
        ("x", 2, lambda i: [box(b0 + (low * NY + y) * r0, r0, (high * NX + i) * LANES, LANES)]),
        ("y", 2, lambda i: [box(b0 + (low * NY + i) * r0, r0, high * NX * LANES, NX * LANES)]),
        ("z", 4, lambda i: [box(b0 + (i % NL) * NY * r0, NY * r0, (i // NL) * NX * LANES, NX * LANES)]),
    )
    second = (
        ("y", 2, lambda i: [box(b1 + (low * NY + i) * r1, r1, column(z, x), LANES)]),
        ("z", 2, lambda i: [box(b1 + (i % NL) * NY * r1, NY * r1, column(i, x), LANES)]),
        ("x", 2, lambda i: [box(b1, 16 * r1, (h * NX + i) * LANES, LANES) for h in range(2)]),
    )
    third = (
        ("z", 2, lambda i: [box(b2 + (y * NL + i % NL) * r2, r2, column(i, x), LANES)]),
        ("x", 1, lambda i: [box(b2 + y * NL * r2, NL * r2, (h * NX + i) * LANES, LANES) for h in range(2)]),
        ("y", 4, lambda i: [box(b2 + i * NL * r2, NL * r2, 0, 2 * NX * LANES)]),
    )
    own = (
        (0, r0, aligned(b0 + (low * NY + y) * r0, 16)),
        (r0, r1, aligned(b1 + (low * NY + y) * r1, 16)),
        (r0 + r1, r2, aligned(b2 + (y * NL + low) * r2, 16)),
    )
    return (first, second, third), own, aligned(column(z, x), LANES)


def pieces(boxes, cuts):
    out = []
    for row, count, col, width in boxes:
        start = 0
        for left in range(cuts, 0, -1):
            size = ((count - start) // 16 + left - 1) // left * 16
            out.append((aligned(row + start, 16), size, col, width))
            start += size
    return out


def ring_sends(plans, position, size):
    sends, free = [], {}
    hop, rate = 1.7, 45.0e3
    for colour, stages in enumerate(plans):
        before = []
        for axis, cuts, boxes in stages:
            n, me = size[axis], position[axis]
            now, chain = [], {}
            for s in range(1, n // 2 + 1):
                for way in (1, -1):
                    out = pieces(boxes((me - way * (s - 1) + n) % n), cuts)
                    got = pieces(boxes((me - way * s + n) % n), cuts)
                    middle = len(out) // 2
                    keep = range(len(out))
                    if s == n // 2:
                        keep = keep[:middle] if way == 1 else keep[middle:]
                    for p in keep:
                        needs = before if s == 1 else [chain[way, s - 1, p]]
                        chain[way, s, p] = len(sends)
                        now.append(len(sends))
                        sends.append((colour, axis, way, out[p], got[p], needs))
            before = now
    order, left, arrive = [], set(range(len(sends))), {}
    while left:
        best = None
        for i in left:
            needs = sends[i][5]
            if all(n in arrive for n in needs):
                start = max([arrive[n] for n in needs] + [0.0])
                key = (max(start, free.get(sends[i][1:3], 0.0)), start, i)
                if best is None or key < best:
                    best = key
        at, start, i = best
        left.remove(i)
        _, count, _, width = sends[i][3]
        free[sends[i][1:3]] = at + count * width * 2 / rate
        arrive[i] = at + count * width * 2 / rate + hop
        order.append((start, i))
    order.sort()
    return sends, [i for _, i in order]


def cluster(
    rows, chunk, inverse, scale_up, value, weighted_ref, counts_ref,
    embed, cents, expo, prob, maxima, logs, total, heard, other_sum, own_sum, kept_sum, tally, other_count, sent_count,
    send_sem, recv_sem, lse_send, lse_recv, out_sem,
):
    x, y, z, core = coordinates()
    here = {"x": x, "y": y, "z": z}
    size = {"x": NX, "y": NY, "z": NZ}
    mate = device(x, y, z, 1 - core)
    per = weighted_ref.shape[0]
    mine, theirs = aligned(core * per, 256), aligned((1 - core) * per, 256)

    def at(axis, value):
        place = dict(here)
        place[axis] = value
        return device(place["x"], place["y"], place["z"], core)

    colours, own, own_col = gather_plan(rows, x, y, z)
    for start, count, row in own:
        embed[pl.ds(row, count), pl.ds(own_col, LANES)] = value[start:start + count]

    def view(box):
        row, count, col, width = box
        return embed.at[pl.ds(row, count), pl.ds(col, width)]

    sends, order = ring_sends(colours, here, size)
    arrived, sent = set(), []

    def remote(i, piece):
        _, axis, way = sends[i][:3]
        return pltpu.make_async_remote_copy(
            src_ref=view(piece), dst_ref=view(piece), send_sem=send_sem.at[i], recv_sem=recv_sem.at[i],
            device_id=at(axis, (here[axis] + way + size[axis]) % size[axis]), device_id_type=MESH)

    def hear(i):
        if i not in arrived:
            arrived.add(i)
            remote(i, sends[i][4]).wait_recv()

    for i in order:
        for need in sends[i][5]:
            hear(need)
        copy = remote(i, sends[i][3])
        copy.start()
        sent.append(copy)

    groups, start = [], 0
    for r in rows:
        groups.append((start, NY * NL * r))
        start += NY * NL * r

    def score(g):
        start, count = groups[g]
        span = pl.ds(start, count)
        scores = lax.dot_general(
            cents[...], embed[span, :], (((1,), (1,)), ((), ())), preferred_element_type=jnp.float32
        ) * inverse
        top = jnp.max(scores, axis=0, keepdims=True)
        powers = jnp.exp(scores - top)
        expo[:, span] = powers
        maxima[:, span] = top
        logs[:, span] = top + jnp.log(jnp.sum(powers, axis=0, keepdims=True))

    bases = {"x": 0, "y": NX - 1, "z": NX + NY - 2}

    def exchange(g, stage):
        axis, span = "xyz"[stage], pl.ds(*groups[g])
        source = (logs if stage == 0 else total.at[stage - 1]).at[:, span]
        copies = []
        for i in range(1, size[axis]):
            slot = bases[axis] + i - 1
            copies.append(pltpu.make_async_remote_copy(
                src_ref=source, dst_ref=heard.at[slot, :, span], send_sem=lse_send.at[g, slot],
                recv_sem=lse_recv.at[g, slot], device_id=at(axis, (here[axis] + i) % size[axis]),
                device_id_type=MESH))
        return source, copies

    def tell(g, stage):
        for copy in exchange(g, stage)[1]:
            copy.start()
            sent.append(copy)

    def learn(g, stage):
        source, copies = exchange(g, stage)
        span = pl.ds(*groups[g])
        for copy in copies:
            copy.wait_recv()
        base = bases["xyz"[stage]]
        parts = [source[...]] + [heard[base + i, :, span] for i in range(len(copies))]
        top = functools.reduce(jnp.maximum, parts)
        total[stage, :, span] = top + jnp.log(sum(jnp.exp(p - top) for p in parts))

    def weigh(g):
        start, count = groups[g]
        whole = pl.ds(start, count)
        maxima[:, whole] = jnp.exp(maxima[:, whole] - total[2, :, whole])

        def step(i, running):
            span = pl.ds(aligned(start + i * chunk, chunk), chunk)
            p = expo[:, span] * maxima[:, span]
            prob[:, span] = p.astype(jnp.bfloat16)
            return running + sum(p[:, j * LANES:(j + 1) * LANES] for j in range(chunk // LANES))

        first = jnp.zeros(tally.shape, jnp.float32) if g == 0 else tally[...]
        tally[...] = lax.fori_loop(0, count // chunk, step, first)

    lanes = 256

    def product(g, first, j):
        start, count = groups[g]
        return lax.dot_general(
            prob[pl.ds(first, per), pl.ds(start, count)], embed[pl.ds(start, count), j * lanes:(j + 1) * lanes],
            (((1,), (0,)), ((), ())), preferred_element_type=jnp.float32)

    blocks = embed.shape[1] // lanes

    def accumulate(g):
        for j in range(blocks):
            cols = pl.ds(j * lanes, lanes)
            for first, ref in ((theirs, own_sum), (mine, kept_sum)):
                value = product(g, first, j)
                ref[:, cols] = value if g == 0 else ref[:, cols] + value

    def ends(c):
        for i in order:
            if sends[i][0] == c:
                hear(i)

    ends(0)
    score(0)
    tell(0, 0)
    ends(1)
    score(1)
    tell(1, 0)
    learn(0, 0)
    tell(0, 1)
    ends(2)
    score(2)
    tell(2, 0)
    learn(1, 0)
    tell(1, 1)
    learn(0, 1)
    tell(0, 2)
    learn(2, 0)
    tell(2, 1)
    learn(1, 1)
    tell(1, 2)
    learn(0, 2)
    weigh(0)
    learn(2, 1)
    tell(2, 2)
    accumulate(0)
    learn(1, 2)
    weigh(1)
    accumulate(1)
    learn(2, 2)
    weigh(2)
    sent_count[...] = scale_up * jnp.sum(tally[...].T, axis=0, keepdims=True)

    give = [pltpu.make_async_remote_copy(
        src_ref=sent_count, dst_ref=other_count, send_sem=out_sem.at[0, blocks],
        recv_sem=out_sem.at[1, blocks], device_id=mate, device_id_type=MESH)]
    give[0].start()
    for j in range(blocks):
        cols = pl.ds(j * lanes, lanes)
        own_sum[:, cols] = scale_up * (own_sum[:, cols] + product(2, theirs, j))
        give.append(pltpu.make_async_remote_copy(
            src_ref=own_sum.at[:, cols], dst_ref=other_sum.at[:, cols], send_sem=out_sem.at[0, j],
            recv_sem=out_sem.at[1, j], device_id=mate, device_id_type=MESH))
        give[-1].start()
    for j in range(blocks):
        cols = pl.ds(j * lanes, lanes)
        part = scale_up * (kept_sum[:, cols] + product(2, mine, j))
        give[1 + j].wait_recv()
        part = part + other_sum[:, cols]
        for b in range(lanes // LANES):
            q = j * (lanes // LANES) + b
            c = (q % NX) * 2 + q // NX
            weighted_ref[:, c * LANES:(c + 1) * LANES] = part[:, b * LANES:(b + 1) * LANES]
    give[0].wait_recv()
    counts_ref[...] = sent_count[:, pl.ds(mine, per)] + other_count[:, pl.ds(mine, per)]
    for copy in give + sent:
        copy.wait_send()


def encode(
    early, later, hidden_ref, residual_ref, down_ref, gain_ref, proj_ref,
    down, hid, res, scale, proj, part, relayed, heard, layer, heard_f, normed, turned,
    sums_x, relayed_x, heard_x, sums_h, heard_h, square, squares,
    send_sem, recv_sem, local_sem, part_send, part_recv, z_send, z_recv, far_send, far_recv,
):
    x, y, z, core = coordinates()
    low, high = z % NL, z // NL
    mate = device(x, y, z, 1 - core)
    far = device(x, y, (z + NL) % NZ, core)
    turn = device(y, x, z, core)
    alone = x == y

    def at_x(i):
        return device((x + i) % NX, y, z, core)

    def at_far(i):
        return device((x + i) % NX, y, (z + NL) % NZ, core)

    def at_y(i):
        return device(x, (y + i) % NY, z, core)

    peers = [mate] + [f(i) for f in (at_x, at_far, at_y) for i in (1, 2, 3)]
    peers += [device(x, y, (z + i) % NZ, core) for i in range(1, NZ)]
    barrier = pltpu.get_barrier_semaphore()
    for peer in peers:
        pl.semaphore_signal(barrier, inc=1, device_id=peer, device_id_type=MESH)

    @pl.when(jnp.logical_not(alone))
    def _():
        pl.semaphore_signal(barrier, inc=1, device_id=turn, device_id_type=MESH)

    pl.semaphore_wait(barrier, jnp.where(alone, len(peers), len(peers) + 1))

    used, done, kept = [0], [], []

    def remote(src, dst, target, start=True):
        i = used[0]
        used[0] += 1
        copy = pltpu.make_async_remote_copy(
            src_ref=src, dst_ref=dst, send_sem=send_sem.at[i], recv_sem=recv_sem.at[i],
            device_id=target, device_id_type=MESH)
        if start:
            copy.start()
            done.append(copy)
        return copy

    def local(src, dst, start=True):
        copy = pltpu.make_async_copy(src, dst, local_sem.at[len(kept)])
        kept.append(copy)
        if start:
            copy.start()
        return copy

    def transposed(src, dst):
        out, here = remote(src, dst, turn, False), local(src, dst, False)

        @pl.when(jnp.logical_not(alone))
        def _():
            out.start()

        @pl.when(alone)
        def _():
            here.start()

        return out, here

    def land(pair):
        @pl.when(jnp.logical_not(alone))
        def _():
            pair[0].wait()

        @pl.when(alone)
        def _():
            pair[1].wait()

    mine = pl.ds(aligned(core * LANES, LANES), LANES)
    passages = hidden_ref.shape[0]
    wide = 2 * LANES

    own = down.at[low, :, mine]
    near = [low, low + 1 - 2 * (low % 2), jnp.where(low < 2, 2, 1), jnp.where(low < 2, 3, 0)]

    def along_z(source, target):
        block = down.at[source, :, mine]
        return pltpu.make_async_remote_copy(
            src_ref=down_ref, dst_ref=block, send_sem=z_send.at[target], recv_sem=z_recv.at[source],
            device_id=device(x, y, high * NL + target, core), device_id_type=MESH)

    for target in near[1:]:
        along_z(low, target).start()
    along_y = [remote(hidden_ref, hid.at[y], at_y(i)) for i in (1, 3)]
    crossed = {0: remote(down_ref, own, mate)}
    first = [local(down_ref, own), local(hidden_ref, hid.at[y])]
    loaded = local(proj_ref, proj)
    moved = [transposed(residual_ref, res), transposed(gain_ref, scale)]
    early()

    for copy in along_y:
        copy.wait_recv()
    upper = (passages // 2 + 15) // 16 * 16
    lower = hid.at[(y + 3) % NY, pl.ds(0, upper), :]
    along_y = [remote(lower, lower, at_y(1))]
    lower = hid.at[(y + 1) % NY, pl.ds(upper, passages - upper), :]
    along_y.append(remote(lower, lower, at_y(3)))
    for copy in first:
        copy.wait()
    for copy in along_y:
        copy.wait_recv()
    flat = (NY * passages, hid.shape[2])
    sent = []
    cut = passages // 2
    spans = (pl.ds(0, cut), pl.ds(cut, passages - cut))

    def scatter(view, relay, got, send, recv):
        def copies(i):
            way = 1 if i % 2 == 0 else 3
            if i < 2:
                src, dst = view((x + 2) % NX).at[spans[i], :], relay(i)
            else:
                src, dst = view((x + way) % NX), got(i - 2)
            return pltpu.make_async_remote_copy(
                src_ref=src, dst_ref=dst, send_sem=send(i), recv_sem=recv(i),
                device_id=at_x(way), device_id_type=MESH)

        def start(i):
            copy = copies(i)
            copy.start()
            sent.append(copy)

        def first():
            start(0)
            start(1)

        def second():
            for i, way in ((0, 1), (1, 3)):
                copies(i).wait_recv()
                target = view((x + way) % NX)
                target[spans[i], :] = target[spans[i], :] + relay(i)[...]
                start(2 + i)

        def finish():
            copies(2).wait_recv()
            copies(3).wait_recv()
            return view(x)[...] + got(0)[...] + got(1)[...]

        return first, second, finish

    def block_scatter(zc):
        return scatter(
            lambda q: part.at[zc, q], lambda i: relayed.at[zc, i], lambda i: heard.at[zc, i],
            lambda i: part_send.at[zc, i], lambda i: part_recv.at[zc, i])

    def far_copy(zc):
        return pltpu.make_async_remote_copy(
            src_ref=layer.at[zc], dst_ref=heard_f.at[zc % 2], send_sem=far_send.at[zc % 2],
            recv_sem=far_recv.at[zc % 2], device_id=far, device_id_type=MESH)

    def third(zc):
        layer[zc] = block_scatter(zc)[2]()

        @pl.when(zc // 2 != high)
        def _():
            far_copy(zc).start()

    for n, zc in enumerate(near):
        if n:
            along_z(zc, zc).wait_recv()
            crossed[n] = remote(down.at[zc, :, mine], down.at[zc, :, mine], mate)
        crossed[n].wait_recv()
        value = jnp.dot(hid[...].reshape(flat), down[zc], preferred_element_type=jnp.float32)
        for q in range(NX):
            part[zc, q] = value[q * passages:(q + 1) * passages]
        block_scatter(zc)[0]()
        if n > 0:
            block_scatter(near[n - 1])[1]()
        if n > 1:
            third(near[n - 2])
    block_scatter(near[3])[1]()
    third(near[2])
    third(near[3])

    later()
    for pair in moved:
        land(pair)
    for b in range(2):
        value = layer[high * 2 + b]
        far_copy(high * 2 + b).wait_recv()
        cols = pl.ds(b * wide, wide)
        gain = jnp.concatenate([scale[2 * b], scale[2 * b + 1]], axis=1)
        value = value + heard_f[b] + res[:, cols].astype(jnp.float32)
        normed[:, cols] = (value * gain).astype(jnp.bfloat16)
    land(transposed(normed, turned))
    loaded.wait()
    mixed = jnp.dot(turned[...], proj[...], preferred_element_type=jnp.float32)
    for q in range(NX):
        sums_x[q] = mixed[:, q * wide:(q + 1) * wide]
    first, second, finish = scatter(
        lambda q: sums_x.at[q], lambda i: relayed_x.at[i], lambda i: heard_x.at[i],
        lambda i: part_send.at[NL, i], lambda i: part_recv.at[NL, i])
    first()
    second()
    value = finish()
    for h in range(2):
        sums_h[h] = value[:, h * LANES:(h + 1) * LANES]
    remote(sums_h.at[1 - high], heard_h, far).wait_recv()
    value = sums_h[high] + heard_h[...]

    pad = square.shape[1] - passages
    squared = jnp.concatenate([value * value, jnp.zeros((pad, LANES), jnp.float32)], axis=0)
    square[...] = jnp.sum(squared.T, axis=0, keepdims=True)
    stage = [remote(square, squares.at[i - 1], at_x(i)) for i in (1, 2, 3)]
    stage += [remote(square, squares.at[3 + i], at_far(i)) for i in range(4)]
    for copy in stage:
        copy.wait_recv()
    total = square[...]
    for i in range(7):
        total = total + squares[i]
    norm = lax.rsqrt(total * (1.0 / proj_ref.shape[1]) + 1e-06)
    norm = jnp.broadcast_to(norm, (LANES, norm.shape[1])).T
    for target in near[1:]:
        along_z(low, target).wait_send()
    for b in range(2):
        far_copy((1 - high) * 2 + b).wait_send()
    for copy in sent + done:
        copy.wait_send()
    return (value * norm[:passages]).astype(jnp.bfloat16)


def whole_kernel(
    split, plan, hidden_ref, residual_ref, down_ref, gain_ref, proj_ref, cent_ref, weighted_ref, counts_ref, *scratch,
):
    cent_local, cent_sem, *scratch = scratch
    encoder, rest = scratch[:split], scratch[split:]
    cents = rest[1]
    x, y, z, core = coordinates()
    per = cent_ref.shape[0]
    mine, theirs = (pl.ds(aligned(c * per, 256), per) for c in (core, 1 - core))

    def shared(rows):
        return pltpu.make_async_remote_copy(
            src_ref=cents.at[rows, :], dst_ref=cents.at[rows, :], send_sem=cent_sem.at[0],
            recv_sem=cent_sem.at[1], device_id=device(x, y, z, 1 - core), device_id_type=MESH)

    copies = [
        pltpu.make_async_copy(
            cent_ref.at[:, pl.ds(c * LANES, LANES)],
            cents.at[mine, pl.ds(((c % 2) * NX + c // 2) * LANES, LANES)],
            cent_local.at[c])
        for c in range(2 * NX)
    ]

    def early():
        for copy in copies:
            copy.start()

    def later():
        for copy in copies:
            copy.wait()
        shared(mine).start()

    value = encode(early, later, hidden_ref, residual_ref, down_ref, gain_ref, proj_ref, *encoder)
    shared(theirs).wait_recv()
    shared(mine).wait_send()
    cluster(*plan, value, weighted_ref, counts_ref, *rest)


def body(hidden, residual, down_weight, gain, proj_weight, centroids):
    passages, units = hidden.shape
    features, embed_width = proj_weight.shape
    per = centroids.shape[0]
    everyone = passages * lax.axis_size("dp")
    centres = per * lax.axis_size("dp") * lax.axis_size("cent")
    r0 = passages // 3 // 16 * 16
    r1 = (passages - r0) // 32 * 16
    rows = (r0, r1, passages - r0 - r1)
    count = everyone // 2
    bf16, f32 = jnp.bfloat16, jnp.float32
    vmem = pl.BlockSpec(memory_space=pltpu.VMEM)
    hbm = pl.BlockSpec(memory_space=pl.ANY)
    wide = 2 * LANES
    padded = (passages + LANES - 1) // LANES * LANES
    slots = 3 + 4 + 4 + 3 + 2 + 1 + 7
    hops = NX + NY + NZ - 3
    encoder = [
        pltpu.VMEM((NL, units, wide), bf16),
        pltpu.VMEM((NY, passages, units), bf16),
        pltpu.VMEM((passages, features), bf16),
        pltpu.VMEM((features // LANES, 1, LANES), f32),
        pltpu.VMEM((features, embed_width), bf16),
        pltpu.VMEM((NL, NX, passages, wide), f32),
        pltpu.VMEM((NL, 2, passages // 2, wide), f32),
        pltpu.VMEM((NL, 2, passages, wide), f32),
        pltpu.VMEM((NL, passages, wide), f32),
        pltpu.VMEM((2, passages, wide), f32),
        pltpu.VMEM((passages, features), bf16),
        pltpu.VMEM((passages, features), bf16),
        pltpu.VMEM((NX, passages, wide), f32),
        pltpu.VMEM((2, passages // 2, wide), f32),
        pltpu.VMEM((2, passages, wide), f32),
        pltpu.VMEM((2, passages, LANES), f32),
        pltpu.VMEM((passages, LANES), f32),
        pltpu.VMEM((1, padded), f32),
        pltpu.VMEM((7, 1, padded), f32),
        pltpu.SemaphoreType.DMA((slots,)),
        pltpu.SemaphoreType.DMA((slots,)),
        pltpu.SemaphoreType.DMA((6,)),
        pltpu.SemaphoreType.DMA((NL + 1, 4)),
        pltpu.SemaphoreType.DMA((NL + 1, 4)),
        pltpu.SemaphoreType.DMA((NL,)),
        pltpu.SemaphoreType.DMA((NL,)),
        pltpu.SemaphoreType.DMA((2,)),
        pltpu.SemaphoreType.DMA((2,)),
    ]
    rest = [
        pltpu.VMEM((count, embed_width), bf16),
        pltpu.VMEM((2 * per, embed_width), bf16),
        pltpu.VMEM((2 * per, count), f32),
        pltpu.VMEM((2 * per, count), bf16),
        pltpu.VMEM((1, count), f32),
        pltpu.VMEM((1, count), f32),
        pltpu.VMEM((3, 1, count), f32),
        pltpu.VMEM((hops, 1, count), f32),
        pltpu.VMEM((per, embed_width), f32),
        pltpu.VMEM((per, embed_width), f32),
        pltpu.VMEM((per, embed_width), f32),
        pltpu.VMEM((2 * per, LANES), f32),
        pltpu.VMEM((1, 2 * per), f32),
        pltpu.VMEM((1, 2 * per), f32),
        pltpu.SemaphoreType.DMA((128,)),
        pltpu.SemaphoreType.DMA((128,)),
        pltpu.SemaphoreType.DMA((3, hops)),
        pltpu.SemaphoreType.DMA((3, hops)),
        pltpu.SemaphoreType.DMA((2, 5)),
    ]
    plan = (rows, 256, 1.0 / (math.sqrt(embed_width) * 0.05), centres / everyone)
    weighted, counts = pl.pallas_call(
        functools.partial(whole_kernel, len(encoder), plan),
        out_shape=(jax.ShapeDtypeStruct((per, embed_width), f32), jax.ShapeDtypeStruct((1, per), f32)),
        in_specs=[hbm] * 6,
        out_specs=(vmem, vmem),
        scratch_shapes=[pltpu.SemaphoreType.DMA((2 * NX,)), pltpu.SemaphoreType.DMA((2,))] + encoder + rest,
        compiler_params=pltpu.CompilerParams(
            collective_id=0, has_side_effects=True, vmem_limit_bytes=63 * 1024 * 1024),
        name="soft_kmeans",
    )(hidden, residual, down_weight, gain.reshape(features // LANES, 1, LANES), proj_weight, centroids)
    return weighted, counts.reshape(per)


def solution(mesh):
    in_specs = (
        P("dp", "cent"),
        P("dp", "cent"),
        P("cent", "dp"),
        P("cent"),
        P("cent", None),
        P(("dp", "cent"), None),
    )
    out_specs = (P(("dp", "cent"), None), P(("dp", "cent")))
    return jax.shard_map(body, mesh=mesh, in_specs=in_specs, out_specs=out_specs, check_vma=False)
```

```python
import functools
import math

import jax
import jax.numpy as jnp
from jax import lax
from jax.experimental import pallas as pl
from jax.experimental.pallas import tpu as pltpu
from jax.sharding import PartitionSpec as P

MESH = pl.DeviceIdType.MESH
NX, NY, NZ = 4, 4, 8
NL = 4
LANES = 128


def coordinates():
    dp, cent = lax.axis_index("dp"), lax.axis_index("cent")
    y, low, core = dp // (2 * NL), (dp // 2) % NL, dp % 2
    return cent // 2, y, (cent % 2) * NL + low, core


def device(x, y, z, core):
    return (y * (2 * NL) + (z % NL) * 2 + core, x * 2 + z // NL)


def aligned(value, multiple):
    return pl.multiple_of(value, multiple)


def gather_plan(rows, x, y, z):
    low, high = z % NL, z // NL
    r0, r1, r2 = rows
    b0, b1, b2 = 0, 16 * r0, 16 * (r0 + r1)

    def box(row, count, col, width):
        return (aligned(row, 16), count, aligned(col, LANES), width)

    def column(zc, xc):
        return ((zc // NL) * NX + xc) * LANES

    first = (
        ("x", 2, lambda i: [box(b0 + (low * NY + y) * r0, r0, (high * NX + i) * LANES, LANES)]),
        ("y", 2, lambda i: [box(b0 + (low * NY + i) * r0, r0, high * NX * LANES, NX * LANES)]),
        ("z", 4, lambda i: [box(b0 + (i % NL) * NY * r0, NY * r0, (i // NL) * NX * LANES, NX * LANES)]),
    )
    second = (
        ("y", 2, lambda i: [box(b1 + (low * NY + i) * r1, r1, column(z, x), LANES)]),
        ("z", 2, lambda i: [box(b1 + (i % NL) * NY * r1, NY * r1, column(i, x), LANES)]),
        ("x", 2, lambda i: [box(b1, 16 * r1, (h * NX + i) * LANES, LANES) for h in range(2)]),
    )
    third = (
        ("z", 2, lambda i: [box(b2 + (y * NL + i % NL) * r2, r2, column(i, x), LANES)]),
        ("x", 1, lambda i: [box(b2 + y * NL * r2, NL * r2, (h * NX + i) * LANES, LANES) for h in range(2)]),
        ("y", 4, lambda i: [box(b2 + i * NL * r2, NL * r2, 0, 2 * NX * LANES)]),
    )
    own = (
        (0, r0, aligned(b0 + (low * NY + y) * r0, 16)),
        (r0, r1, aligned(b1 + (low * NY + y) * r1, 16)),
        (r0 + r1, r2, aligned(b2 + (y * NL + low) * r2, 16)),
    )
    return (first, second, third), own, aligned(column(z, x), LANES)


def pieces(boxes, cuts):
    out = []
    for row, count, col, width in boxes:
        start = 0
        for left in range(cuts, 0, -1):
            size = ((count - start) // 16 + left - 1) // left * 16
            out.append((aligned(row + start, 16), size, col, width))
            start += size
    return out


def ring_sends(plans, position, size):
    sends, free = [], {}
    hop, rate = 1.7, 45.0e3
    for colour, stages in enumerate(plans):
        before = []
        for axis, cuts, boxes in stages:
            n, me = size[axis], position[axis]
            now, chain = [], {}
            for s in range(1, n // 2 + 1):
                for way in (1, -1):
                    out = pieces(boxes((me - way * (s - 1) + n) % n), cuts)
                    got = pieces(boxes((me - way * s + n) % n), cuts)
                    middle = len(out) // 2
                    keep = range(len(out))
                    if s == n // 2:
                        keep = keep[:middle] if way == 1 else keep[middle:]
                    for p in keep:
                        needs = before if s == 1 else [chain[way, s - 1, p]]
                        chain[way, s, p] = len(sends)
                        now.append(len(sends))
                        sends.append((colour, axis, way, out[p], got[p], needs))
            before = now
    order, left, arrive = [], set(range(len(sends))), {}
    while left:
        best = None
        for i in left:
            needs = sends[i][5]
            if all(n in arrive for n in needs):
                start = max([arrive[n] for n in needs] + [0.0])
                key = (max(start, free.get(sends[i][1:3], 0.0)), start, i)
                if best is None or key < best:
                    best = key
        at, start, i = best
        left.remove(i)
        _, count, _, width = sends[i][3]
        free[sends[i][1:3]] = at + count * width * 2 / rate
        arrive[i] = at + count * width * 2 / rate + hop
        order.append((start, i))
    order.sort()
    return sends, [i for _, i in order]


def cluster(
    rows, chunk, inverse, scale_up, value, weighted_ref, counts_ref,
    embed, cents, expo, prob, maxima, logs, total, heard, other_sum, own_sum, kept_sum, tally, other_count, sent_count,
    send_sem, recv_sem, lse_send, lse_recv, out_sem,
):
    x, y, z, core = coordinates()
    here = {"x": x, "y": y, "z": z}
    size = {"x": NX, "y": NY, "z": NZ}
    mate = device(x, y, z, 1 - core)
    per = weighted_ref.shape[0]
    mine, theirs = aligned(core * per, 256), aligned((1 - core) * per, 256)

    def at(axis, value):
        place = dict(here)
        place[axis] = value
        return device(place["x"], place["y"], place["z"], core)

    colours, own, own_col = gather_plan(rows, x, y, z)
    for start, count, row in own:
        embed[pl.ds(row, count), pl.ds(own_col, LANES)] = value[start:start + count]

    def view(box):
        row, count, col, width = box
        return embed.at[pl.ds(row, count), pl.ds(col, width)]

    sends, order = ring_sends(colours, here, size)
    arrived, sent = set(), []

    def remote(i, piece):
        _, axis, way = sends[i][:3]
        return pltpu.make_async_remote_copy(
            src_ref=view(piece), dst_ref=view(piece), send_sem=send_sem.at[i], recv_sem=recv_sem.at[i],
            device_id=at(axis, (here[axis] + way + size[axis]) % size[axis]), device_id_type=MESH)

    def hear(i):
        if i not in arrived:
            arrived.add(i)
            remote(i, sends[i][4]).wait_recv()

    for i in order:
        for need in sends[i][5]:
            hear(need)
        copy = remote(i, sends[i][3])
        copy.start()
        sent.append(copy)

    groups, start = [], 0
    for r in rows:
        groups.append((start, NY * NL * r))
        start += NY * NL * r

    def score(g):
        start, count = groups[g]
        span = pl.ds(start, count)
        scores = lax.dot_general(
            cents[...], embed[span, :], (((1,), (1,)), ((), ())), preferred_element_type=jnp.float32
        ) * inverse
        top = jnp.max(scores, axis=0, keepdims=True)
        powers = jnp.exp(scores - top)
        expo[:, span] = powers
        maxima[:, span] = top
        logs[:, span] = top + jnp.log(jnp.sum(powers, axis=0, keepdims=True))

    bases = {"x": 0, "y": NX - 1, "z": NX + NY - 2}

    def exchange(g, stage):
        axis, span = "xyz"[stage], pl.ds(*groups[g])
        source = (logs if stage == 0 else total.at[stage - 1]).at[:, span]
        copies = []
        for i in range(1, size[axis]):
            slot = bases[axis] + i - 1
            copies.append(pltpu.make_async_remote_copy(
                src_ref=source, dst_ref=heard.at[slot, :, span], send_sem=lse_send.at[g, slot],
                recv_sem=lse_recv.at[g, slot], device_id=at(axis, (here[axis] + i) % size[axis]),
                device_id_type=MESH))
        return source, copies

    def tell(g, stage):
        for copy in exchange(g, stage)[1]:
            copy.start()
            sent.append(copy)

    def learn(g, stage):
        source, copies = exchange(g, stage)
        span = pl.ds(*groups[g])
        for copy in copies:
            copy.wait_recv()
        base = bases["xyz"[stage]]
        parts = [source[...]] + [heard[base + i, :, span] for i in range(len(copies))]
        top = functools.reduce(jnp.maximum, parts)
        total[stage, :, span] = top + jnp.log(sum(jnp.exp(p - top) for p in parts))

    def weigh(g):
        start, count = groups[g]
        whole = pl.ds(start, count)
        maxima[:, whole] = jnp.exp(maxima[:, whole] - total[2, :, whole])

        def step(i, running):
            span = pl.ds(aligned(start + i * chunk, chunk), chunk)
            p = expo[:, span] * maxima[:, span]
            prob[:, span] = p.astype(jnp.bfloat16)
            return running + sum(p[:, j * LANES:(j + 1) * LANES] for j in range(chunk // LANES))

        first = jnp.zeros(tally.shape, jnp.float32) if g == 0 else tally[...]
        tally[...] = lax.fori_loop(0, count // chunk, step, first)

    lanes = 256

    def product(g, first, j):
        start, count = groups[g]
        return lax.dot_general(
            prob[pl.ds(first, per), pl.ds(start, count)], embed[pl.ds(start, count), j * lanes:(j + 1) * lanes],
            (((1,), (0,)), ((), ())), preferred_element_type=jnp.float32)

    blocks = embed.shape[1] // lanes

    def accumulate(g):
        for j in range(blocks):
            cols = pl.ds(j * lanes, lanes)
            for first, ref in ((theirs, own_sum), (mine, kept_sum)):
                value = product(g, first, j)
                ref[:, cols] = value if g == 0 else ref[:, cols] + value

    def ends(c):
        for i in order:
            if sends[i][0] == c:
                hear(i)

    ends(0)
    score(0)
    tell(0, 0)
    ends(1)
    score(1)
    tell(1, 0)
    learn(0, 0)
    tell(0, 1)
    ends(2)
    score(2)
    tell(2, 0)
    learn(1, 0)
    tell(1, 1)
    learn(0, 1)
    tell(0, 2)
    learn(2, 0)
    tell(2, 1)
    learn(1, 1)
    tell(1, 2)
    learn(0, 2)
    weigh(0)
    learn(2, 1)
    tell(2, 2)
    accumulate(0)
    learn(1, 2)
    weigh(1)
    accumulate(1)
    learn(2, 2)
    weigh(2)
    sent_count[...] = scale_up * jnp.sum(tally[...].T, axis=0, keepdims=True)

    give = [pltpu.make_async_remote_copy(
        src_ref=sent_count, dst_ref=other_count, send_sem=out_sem.at[0, blocks],
        recv_sem=out_sem.at[1, blocks], device_id=mate, device_id_type=MESH)]
    give[0].start()
    for j in range(blocks):
        cols = pl.ds(j * lanes, lanes)
        own_sum[:, cols] = scale_up * (own_sum[:, cols] + product(2, theirs, j))
        give.append(pltpu.make_async_remote_copy(
            src_ref=own_sum.at[:, cols], dst_ref=other_sum.at[:, cols], send_sem=out_sem.at[0, j],
            recv_sem=out_sem.at[1, j], device_id=mate, device_id_type=MESH))
        give[-1].start()
    for j in range(blocks):
        cols = pl.ds(j * lanes, lanes)
        part = scale_up * (kept_sum[:, cols] + product(2, mine, j))
        give[1 + j].wait_recv()
        part = part + other_sum[:, cols]
        for b in range(lanes // LANES):
            q = j * (lanes // LANES) + b
            c = (q % NX) * 2 + q // NX
            weighted_ref[:, c * LANES:(c + 1) * LANES] = part[:, b * LANES:(b + 1) * LANES]
    give[0].wait_recv()
    counts_ref[...] = sent_count[:, pl.ds(mine, per)] + other_count[:, pl.ds(mine, per)]
    for copy in give + sent:
        copy.wait_send()


def encode(
    early, later, hidden_ref, residual_ref, down_ref, gain_ref, proj_ref,
    down, hid, res, scale, proj, part, relayed, heard, layer, heard_f, normed, turned,
    sums_x, relayed_x, heard_x, sums_h, heard_h, square, squares,
    send_sem, recv_sem, local_sem, part_send, part_recv, z_send, z_recv, far_send, far_recv,
):
    x, y, z, core = coordinates()
    low, high = z % NL, z // NL
    mate = device(x, y, z, 1 - core)
    far = device(x, y, (z + NL) % NZ, core)
    turn = device(y, x, z, core)
    alone = x == y

    def at_x(i):
        return device((x + i) % NX, y, z, core)

    def at_far(i):
        return device((x + i) % NX, y, (z + NL) % NZ, core)

    def at_y(i):
        return device(x, (y + i) % NY, z, core)

    peers = [mate] + [f(i) for f in (at_x, at_far, at_y) for i in (1, 2, 3)]
    peers += [device(x, y, (z + i) % NZ, core) for i in range(1, NZ)]
    barrier = pltpu.get_barrier_semaphore()
    for peer in peers:
        pl.semaphore_signal(barrier, inc=1, device_id=peer, device_id_type=MESH)

    @pl.when(jnp.logical_not(alone))
    def _():
        pl.semaphore_signal(barrier, inc=1, device_id=turn, device_id_type=MESH)

    pl.semaphore_wait(barrier, jnp.where(alone, len(peers), len(peers) + 1))

    used, done, kept = [0], [], []

    def remote(src, dst, target, start=True):
        i = used[0]
        used[0] += 1
        copy = pltpu.make_async_remote_copy(
            src_ref=src, dst_ref=dst, send_sem=send_sem.at[i], recv_sem=recv_sem.at[i],
            device_id=target, device_id_type=MESH)
        if start:
            copy.start()
            done.append(copy)
        return copy

    def local(src, dst, start=True):
        copy = pltpu.make_async_copy(src, dst, local_sem.at[len(kept)])
        kept.append(copy)
        if start:
            copy.start()
        return copy

    def transposed(src, dst):
        out, here = remote(src, dst, turn, False), local(src, dst, False)

        @pl.when(jnp.logical_not(alone))
        def _():
            out.start()

        @pl.when(alone)
        def _():
            here.start()

        return out, here

    def land(pair):
        @pl.when(jnp.logical_not(alone))
        def _():
            pair[0].wait()

        @pl.when(alone)
        def _():
            pair[1].wait()

    mine = pl.ds(aligned(core * LANES, LANES), LANES)
    passages = hidden_ref.shape[0]
    wide = 2 * LANES

    own = down.at[low, :, mine]
    near = [low, low + 1 - 2 * (low % 2), jnp.where(low < 2, 2, 1), jnp.where(low < 2, 3, 0)]

    def along_z(source, target):
        block = down.at[source, :, mine]
        return pltpu.make_async_remote_copy(
            src_ref=down_ref, dst_ref=block, send_sem=z_send.at[target], recv_sem=z_recv.at[source],
            device_id=device(x, y, high * NL + target, core), device_id_type=MESH)

    for target in near[1:]:
        along_z(low, target).start()
    along_y = [remote(hidden_ref, hid.at[y], at_y(i)) for i in (1, 3)]
    crossed = {0: remote(down_ref, own, mate)}
    first = [local(down_ref, own), local(hidden_ref, hid.at[y])]
    loaded = local(proj_ref, proj)
    moved = [transposed(residual_ref, res), transposed(gain_ref, scale)]
    early()

    for copy in along_y:
        copy.wait_recv()
    upper = (passages // 2 + 15) // 16 * 16
    lower = hid.at[(y + 3) % NY, pl.ds(0, upper), :]
    along_y = [remote(lower, lower, at_y(1))]
    lower = hid.at[(y + 1) % NY, pl.ds(upper, passages - upper), :]
    along_y.append(remote(lower, lower, at_y(3)))
    for copy in first:
        copy.wait()
    for copy in along_y:
        copy.wait_recv()
    flat = (NY * passages, hid.shape[2])
    sent = []
    cut = passages // 2
    spans = (pl.ds(0, cut), pl.ds(cut, passages - cut))

    def scatter(view, relay, got, send, recv):
        def copies(i):
            way = 1 if i % 2 == 0 else 3
            if i < 2:
                src, dst = view((x + 2) % NX).at[spans[i], :], relay(i)
            else:
                src, dst = view((x + way) % NX), got(i - 2)
            return pltpu.make_async_remote_copy(
                src_ref=src, dst_ref=dst, send_sem=send(i), recv_sem=recv(i),
                device_id=at_x(way), device_id_type=MESH)

        def start(i):
            copy = copies(i)
            copy.start()
            sent.append(copy)

        def first():
            start(0)
            start(1)

        def second():
            for i, way in ((0, 1), (1, 3)):
                copies(i).wait_recv()
                target = view((x + way) % NX)
                target[spans[i], :] = target[spans[i], :] + relay(i)[...]
                start(2 + i)

        def finish():
            copies(2).wait_recv()
            copies(3).wait_recv()
            return view(x)[...] + got(0)[...] + got(1)[...]

        return first, second, finish

    def block_scatter(zc):
        return scatter(
            lambda q: part.at[zc, q], lambda i: relayed.at[zc, i], lambda i: heard.at[zc, i],
            lambda i: part_send.at[zc, i], lambda i: part_recv.at[zc, i])

    def far_copy(zc):
        return pltpu.make_async_remote_copy(
            src_ref=layer.at[zc], dst_ref=heard_f.at[zc % 2], send_sem=far_send.at[zc % 2],
            recv_sem=far_recv.at[zc % 2], device_id=far, device_id_type=MESH)

    def third(zc):
        layer[zc] = block_scatter(zc)[2]()

        @pl.when(zc // 2 != high)
        def _():
            far_copy(zc).start()

    for n, zc in enumerate(near):
        if n:
            along_z(zc, zc).wait_recv()
            crossed[n] = remote(down.at[zc, :, mine], down.at[zc, :, mine], mate)
        crossed[n].wait_recv()
        value = jnp.dot(hid[...].reshape(flat), down[zc], preferred_element_type=jnp.float32)
        for q in range(NX):
            part[zc, q] = value[q * passages:(q + 1) * passages]
        block_scatter(zc)[0]()
        if n > 0:
            block_scatter(near[n - 1])[1]()
        if n > 1:
            third(near[n - 2])
    block_scatter(near[3])[1]()
    third(near[2])
    third(near[3])

    later()
    for pair in moved:
        land(pair)
    turning = []
    for b in range(2):
        value = layer[high * 2 + b]
        far_copy(high * 2 + b).wait_recv()
        cols = pl.ds(b * wide, wide)
        gain = jnp.concatenate([scale[2 * b], scale[2 * b + 1]], axis=1)
        value = value + heard_f[b] + res[:, cols].astype(jnp.float32)
        normed[:, cols] = (value * gain).astype(jnp.bfloat16)
        turning.append(transposed(normed.at[:, cols], turned.at[:, cols]))
    loaded.wait()
    mixed = 0.0
    for b in range(2):
        cols = pl.ds(b * wide, wide)
        land(turning[b])
        mixed = mixed + jnp.dot(turned[:, cols], proj[cols, :], preferred_element_type=jnp.float32)
    for q in range(NX):
        sums_x[q] = mixed[:, q * wide:(q + 1) * wide]
    first, second, finish = scatter(
        lambda q: sums_x.at[q], lambda i: relayed_x.at[i], lambda i: heard_x.at[i],
        lambda i: part_send.at[NL, i], lambda i: part_recv.at[NL, i])
    first()
    second()
    value = finish()
    for h in range(2):
        sums_h[h] = value[:, h * LANES:(h + 1) * LANES]
    remote(sums_h.at[1 - high], heard_h, far).wait_recv()
    value = sums_h[high] + heard_h[...]

    pad = square.shape[1] - passages
    squared = jnp.concatenate([value * value, jnp.zeros((pad, LANES), jnp.float32)], axis=0)
    square[...] = jnp.sum(squared.T, axis=0, keepdims=True)
    stage = [remote(square, squares.at[i - 1], at_x(i)) for i in (1, 2, 3)]
    stage += [remote(square, squares.at[3 + i], at_far(i)) for i in range(4)]
    for copy in stage:
        copy.wait_recv()
    total = square[...]
    for i in range(7):
        total = total + squares[i]
    norm = lax.rsqrt(total * (1.0 / proj_ref.shape[1]) + 1e-06)
    norm = jnp.broadcast_to(norm, (LANES, norm.shape[1])).T
    for target in near[1:]:
        along_z(low, target).wait_send()
    for b in range(2):
        far_copy((1 - high) * 2 + b).wait_send()
    for copy in sent + done:
        copy.wait_send()
    return (value * norm[:passages]).astype(jnp.bfloat16)


def whole_kernel(
    split, plan, hidden_ref, residual_ref, down_ref, gain_ref, proj_ref, cent_ref, weighted_ref, counts_ref, *scratch,
):
    cent_local, cent_sem, *scratch = scratch
    encoder, rest = scratch[:split], scratch[split:]
    cents = rest[1]
    x, y, z, core = coordinates()
    per = cent_ref.shape[0]
    mine, theirs = (pl.ds(aligned(c * per, 256), per) for c in (core, 1 - core))

    def shared(rows):
        return pltpu.make_async_remote_copy(
            src_ref=cents.at[rows, :], dst_ref=cents.at[rows, :], send_sem=cent_sem.at[0],
            recv_sem=cent_sem.at[1], device_id=device(x, y, z, 1 - core), device_id_type=MESH)

    copies = [
        pltpu.make_async_copy(
            cent_ref.at[:, pl.ds(c * LANES, LANES)],
            cents.at[mine, pl.ds(((c % 2) * NX + c // 2) * LANES, LANES)],
            cent_local.at[c])
        for c in range(2 * NX)
    ]

    def early():
        for copy in copies:
            copy.start()

    def later():
        for copy in copies:
            copy.wait()
        shared(mine).start()

    value = encode(early, later, hidden_ref, residual_ref, down_ref, gain_ref, proj_ref, *encoder)
    shared(theirs).wait_recv()
    shared(mine).wait_send()
    cluster(*plan, value, weighted_ref, counts_ref, *rest)


def body(hidden, residual, down_weight, gain, proj_weight, centroids):
    passages, units = hidden.shape
    features, embed_width = proj_weight.shape
    per = centroids.shape[0]
    everyone = passages * lax.axis_size("dp")
    centres = per * lax.axis_size("dp") * lax.axis_size("cent")
    r0 = passages // 3 // 16 * 16
    r1 = (passages - r0) // 32 * 16
    rows = (r0, r1, passages - r0 - r1)
    count = everyone // 2
    bf16, f32 = jnp.bfloat16, jnp.float32
    vmem = pl.BlockSpec(memory_space=pltpu.VMEM)
    hbm = pl.BlockSpec(memory_space=pl.ANY)
    wide = 2 * LANES
    padded = (passages + LANES - 1) // LANES * LANES
    slots = 4 + 4 + 4 + 3 + 2 + 1 + 7
    hops = NX + NY + NZ - 3
    encoder = [
        pltpu.VMEM((NL, units, wide), bf16),
        pltpu.VMEM((NY, passages, units), bf16),
        pltpu.VMEM((passages, features), bf16),
        pltpu.VMEM((features // LANES, 1, LANES), f32),
        pltpu.VMEM((features, embed_width), bf16),
        pltpu.VMEM((NL, NX, passages, wide), f32),
        pltpu.VMEM((NL, 2, passages // 2, wide), f32),
        pltpu.VMEM((NL, 2, passages, wide), f32),
        pltpu.VMEM((NL, passages, wide), f32),
        pltpu.VMEM((2, passages, wide), f32),
        pltpu.VMEM((passages, features), bf16),
        pltpu.VMEM((passages, features), bf16),
        pltpu.VMEM((NX, passages, wide), f32),
        pltpu.VMEM((2, passages // 2, wide), f32),
        pltpu.VMEM((2, passages, wide), f32),
        pltpu.VMEM((2, passages, LANES), f32),
        pltpu.VMEM((passages, LANES), f32),
        pltpu.VMEM((1, padded), f32),
        pltpu.VMEM((7, 1, padded), f32),
        pltpu.SemaphoreType.DMA((slots,)),
        pltpu.SemaphoreType.DMA((slots,)),
        pltpu.SemaphoreType.DMA((7,)),
        pltpu.SemaphoreType.DMA((NL + 1, 4)),
        pltpu.SemaphoreType.DMA((NL + 1, 4)),
        pltpu.SemaphoreType.DMA((NL,)),
        pltpu.SemaphoreType.DMA((NL,)),
        pltpu.SemaphoreType.DMA((2,)),
        pltpu.SemaphoreType.DMA((2,)),
    ]
    rest = [
        pltpu.VMEM((count, embed_width), bf16),
        pltpu.VMEM((2 * per, embed_width), bf16),
        pltpu.VMEM((2 * per, count), f32),
        pltpu.VMEM((2 * per, count), bf16),
        pltpu.VMEM((1, count), f32),
        pltpu.VMEM((1, count), f32),
        pltpu.VMEM((3, 1, count), f32),
        pltpu.VMEM((hops, 1, count), f32),
        pltpu.VMEM((per, embed_width), f32),
        pltpu.VMEM((per, embed_width), f32),
        pltpu.VMEM((per, embed_width), f32),
        pltpu.VMEM((2 * per, LANES), f32),
        pltpu.VMEM((1, 2 * per), f32),
        pltpu.VMEM((1, 2 * per), f32),
        pltpu.SemaphoreType.DMA((128,)),
        pltpu.SemaphoreType.DMA((128,)),
        pltpu.SemaphoreType.DMA((3, hops)),
        pltpu.SemaphoreType.DMA((3, hops)),
        pltpu.SemaphoreType.DMA((2, 5)),
    ]
    plan = (rows, 256, 1.0 / (math.sqrt(embed_width) * 0.05), centres / everyone)
    weighted, counts = pl.pallas_call(
        functools.partial(whole_kernel, len(encoder), plan),
        out_shape=(jax.ShapeDtypeStruct((per, embed_width), f32), jax.ShapeDtypeStruct((1, per), f32)),
        in_specs=[hbm] * 6,
        out_specs=(vmem, vmem),
        scratch_shapes=[pltpu.SemaphoreType.DMA((2 * NX,)), pltpu.SemaphoreType.DMA((2,))] + encoder + rest,
        compiler_params=pltpu.CompilerParams(
            collective_id=0, has_side_effects=True, vmem_limit_bytes=63 * 1024 * 1024),
        name="soft_kmeans",
    )(hidden, residual, down_weight, gain.reshape(features // LANES, 1, LANES), proj_weight, centroids)
    return weighted, counts.reshape(per)


def solution(mesh):
    in_specs = (
        P("dp", "cent"),
        P("dp", "cent"),
        P("cent", "dp"),
        P("cent"),
        P("cent", None),
        P(("dp", "cent"), None),
    )
    out_specs = (P(("dp", "cent"), None), P(("dp", "cent")))
    return jax.shard_map(body, mesh=mesh, in_specs=in_specs, out_specs=out_specs, check_vma=False)
```
